256 devices in a mesh: section: 8 (over z_lo, core), expert: 32 (over y, x, z_hi).
Axes of the slice: x: 4, y: 4, z: 8 (z_hi: 2, z_lo: 4; z = z_hi * 4 + z_lo), core: 2. Of those that a mesh axis runs over, the one named last changes fastest.
Arguments:
- tokens: bfloat16 [8, 4096, 2048], P('section', 'expert'), may hold values from -6 to 6
- routes: int32 [8, 4096, 2], P('section', 'expert'), may hold values from 0 to 15, all different within a row; in each aligned block of 128 rows (0 to 127, 128 to 255, ..., all dimensions but the last counted through in order) at most 32 rows name the same one
- probs: bfloat16 [8, 4096, 2], P('section', 'expert'), may hold values from 0.099609375 to 1
- cotangent: bfloat16 [8, 4096, 2048], P('section', 'expert'), may hold values from -6 to 6
- w_gate: bfloat16 [8, 2048, 12288], P('section', None, 'expert'), may hold values from -0.125 to 0.125
- w_up: bfloat16 [8, 2048, 12288], P('section', None, 'expert'), may hold values from -0.125 to 0.125
- w_down: bfloat16 [8, 12288, 2048], P('section', 'expert'), may hold values from -0.21875 to 0.21875
Outputs:
- upstream: bfloat16 [8, 4096, 2048], P('section', 'expert')
- route_grad: bfloat16 [8, 4096, 2], P('section', 'expert')
- grad_gate: bfloat16 [8, 2048, 12288], P('section', None, 'expert')
- grad_up: bfloat16 [8, 2048, 12288], P('section', None, 'expert')
- grad_down: bfloat16 [8, 12288, 2048], P('section', 'expert')
The draws below stay inside these ranges and needn't reach their ends.
Inputs may be any that keep to these rules, and one draw needn't show every extreme that they name: `routes`: each token names 2 different experts. In each aligned block of 128 rows (the tokens of one device) no expert is named by more than 32 rows, and in some blocks one expert is named by exactly 32 rows.
All inputs are finite; a program needn't handle non-finite values.
Results may differ from the reference program's by a relative error of at most 0.008.
Values may be sent and summed in bfloat16 or wider, within the bound.
A program may use at most 128 MiB of HBM per device.

```python
import math
import jax
import jax.numpy as jnp
import numpy as np
from jax import lax

D = 2048
FF = 768
TOP = 2
TOK_DEV = 128
EXPERTS = 16
CAP = 32
TOKENS = 4096
SECTIONS = 8
N_EXPERT = 32


def level_of(key, shape, split, low, high):
    loudness, own = 1.0, jax.random.fold_in(key, 6)
    for dim, parts in split:
        draws = jnp.exp(jax.random.uniform(jax.random.fold_in(own, dim), (parts,), jnp.float32, low / len(split), high / len(split)))
        loudness = loudness * jnp.repeat(draws, shape[dim] // parts).reshape([-1 if axis == dim else 1 for axis in range(len(shape))])
    return loudness


def routed_block(stream_key, own, number, rows, amount, top, reach, skew):
    ranking = jax.random.permutation(stream_key, amount)
    crowded, ordinary = shares(amount, rows * top, reach, skew, True), shares(amount, rows * top, reach, skew, False)
    places = jnp.arange(amount)

    def named(tallies, rotation):
        used = int((tallies > 0).sum())
        fixed = max(1, used // 4)
        passed = fixed + (places - fixed + rotation * (used - fixed)) % max(1, amount - fixed)
        return jnp.zeros((amount,), jnp.int32).at[ranking[jnp.where(places < fixed, places, passed)]].set(jnp.asarray(tallies, jnp.int32))

    tallies = jnp.where(number % 4 == 0, named(crowded, number // 4), named(ordinary, number - number // 4 - 1))
    mixed = jax.random.permutation(jax.random.fold_in(own, 3), amount)
    donor, receiver = mixed[0:amount // 2 * 2:2], mixed[1:amount // 2 * 2:2]
    slack = jnp.minimum(tallies[donor] - 1, reach - tallies[receiver]) // 2
    slack = jnp.where((donor == ranking[0]) | (receiver == ranking[0]) | (tallies[receiver] == 0), 0, jnp.maximum(slack, 0))
    passed = jax.random.randint(jax.random.fold_in(own, 4), (amount // 2,), 0, 1 << 20) % (slack + 1)
    tallies = tallies.at[donor].add(-passed).at[receiver].add(passed)
    labels = jnp.searchsorted(jnp.cumsum(tallies), jnp.arange(rows * top), side="right").astype(jnp.int32)
    listing = labels.reshape(top, rows).T
    listing = listing[jax.random.permutation(jax.random.fold_in(own, 1), rows)]
    rotation = jax.random.randint(jax.random.fold_in(own, 2), (rows, 1), 0, top)
    return jnp.take_along_axis(listing, (jnp.arange(top)[None, :] + rotation) % top, axis=1)


def shares(number_of, total, reach, skew, full):
    portions = [(1 << 20) // math.isqrt(grade ** skew) + 1 for grade in range(1, number_of + 1)]
    largest = reach if full else min(reach, max(-(-total // number_of), total * portions[0] // sum(portions)))
    least = 1 if total - largest >= number_of - 1 else 0
    counts, rest = [largest] + [least] * (number_of - 1), total - largest - least * (number_of - 1)
    while rest > 0:
        candidates = [i for i in range(1, number_of) if counts[i] < largest] or [i for i in range(1, number_of) if counts[i] < reach]
        mass, left = sum([portions[i] for i in candidates]), rest
        for i in candidates:
            more = min(reach - counts[i], max(1, left * portions[i] // mass), rest)
            counts[i] = counts[i] + more
            rest = rest - more
    return np.array(counts)


def noise(stream_key, dims, width, limit, cuts=(), held_as=jnp.bfloat16):
    level = level_of(stream_key, dims, cuts, -0.22, 0.18) if cuts else 1.0
    drawn = jax.random.normal(stream_key, dims, jnp.float32) * width * level
    return jnp.minimum(jnp.maximum(drawn, -limit), limit).astype(held_as)


def setup_inputs(seed: int = 0) -> dict:
    keys = jax.random.split(jax.random.key(seed), 8)
    tokens = noise(keys[0], (SECTIONS, TOKENS, D), 1.0, 6.0, ((0, 8), (1, 32)))
    routes_keys = jax.random.split(jax.random.fold_in(keys[1], 1), SECTIONS * TOKENS // TOK_DEV)
    routes_turns = jax.random.permutation(jax.random.fold_in(keys[1], 3), SECTIONS * TOKENS // TOK_DEV)
    routes = jax.vmap(lambda own, number: routed_block(jax.random.fold_in(keys[1], 2), own, number, TOK_DEV, EXPERTS, TOP, CAP, 2))(routes_keys, routes_turns).reshape((SECTIONS, TOKENS, TOP))
    probs = jnp.clip(0.099609375 + 0.9003906 * jax.random.uniform(keys[2], (SECTIONS, TOKENS, TOP), jnp.float32) ** level_of(keys[2], (SECTIONS, TOKENS, TOP), ((0, 8), (1, 32)), -0.2, 0.2), 0.099609375, 1.0).astype(jnp.bfloat16)
    cotangent = noise(keys[3], (SECTIONS, TOKENS, D), 1.0, 6.0, ((0, 8), (1, 32)))
    w_gate = noise(keys[4], (SECTIONS, D, EXPERTS * FF), D ** -0.5, 0.125, ((0, 8), (2, 32)))
    w_up = noise(keys[5], (SECTIONS, D, EXPERTS * FF), D ** -0.5, 0.125, ((0, 8), (2, 32)))
    w_down = noise(keys[6], (SECTIONS, EXPERTS * FF, D), FF ** -0.5, 0.21875, ((0, 8), (1, 32)))
    return {"tokens": tokens, "routes": routes, "probs": probs, "cotangent": cotangent, "w_gate": w_gate, "w_up": w_up, "w_down": w_down}


def slot_table(route_rows, experts, capacity):
    flat = route_rows.reshape(-1).astype(jnp.int32)
    count = flat.shape[0]
    onehot = (flat[:, None] == jnp.arange(experts, dtype=jnp.int32)[None, :]).astype(jnp.int32)
    before = jnp.cumsum(onehot, axis=0, dtype=jnp.int32) - onehot
    position = jnp.sum(before * onehot, axis=1, dtype=jnp.int32)
    slot = (flat * capacity + position).astype(jnp.int32)
    owner = jnp.full((experts * capacity,), -1, jnp.int32).at[slot].set(jnp.arange(count, dtype=jnp.int32))
    return slot, owner


def expert_pass(items):
    xin, dyin, pin, wg, wu, wd = items
    pin = pin.astype(jnp.float32)
    gate = jnp.dot(xin, wg, preferred_element_type=jnp.float32)
    up = jnp.dot(xin, wu, preferred_element_type=jnp.float32)
    sig = jax.nn.sigmoid(gate)
    act = gate * sig
    hidden = (act * up).astype(jnp.bfloat16)
    back = lax.dot_general(dyin, wd, (((1,), (1,)), ((), ())), preferred_element_type=jnp.float32)
    route_part = jnp.sum(back * hidden.astype(jnp.float32), axis=1).astype(jnp.bfloat16)
    scaled = pin[:, None] * back
    d_gate = (scaled * up * sig * (1.0 + gate * (1.0 - sig))).astype(jnp.bfloat16)
    d_up = (scaled * act).astype(jnp.bfloat16)
    weighted = (pin[:, None] * hidden.astype(jnp.float32)).astype(jnp.bfloat16)
    g_gate = lax.dot_general(xin, d_gate, (((0,), (0,)), ((), ())), preferred_element_type=jnp.float32).astype(jnp.bfloat16)
    g_up = lax.dot_general(xin, d_up, (((0,), (0,)), ((), ())), preferred_element_type=jnp.float32).astype(jnp.bfloat16)
    g_down = lax.dot_general(weighted, dyin, (((0,), (0,)), ((), ())), preferred_element_type=jnp.float32).astype(jnp.bfloat16)
    part_dx = lax.dot_general(d_gate, wg, (((1,), (1,)), ((), ())), preferred_element_type=jnp.float32)
    part_dx = part_dx + lax.dot_general(d_up, wu, (((1,), (1,)), ((), ())), preferred_element_type=jnp.float32)
    return g_gate, g_up, g_down, part_dx.astype(jnp.bfloat16), route_part


def reference(tokens, routes, probs, cotangent, w_gate, w_up, w_down):
    def pack_source(rows_x, rows_r, rows_p, rows_dy):
        slot, owner = slot_table(rows_r, EXPERTS, CAP)
        valid = owner >= 0
        entry = jnp.maximum(owner, 0)
        token_of = entry // TOP
        send_x = jnp.where(valid[:, None], rows_x[token_of], jnp.zeros((), jnp.bfloat16)).astype(jnp.bfloat16)
        send_dy = jnp.where(valid[:, None], rows_dy[token_of], jnp.zeros((), jnp.bfloat16)).astype(jnp.bfloat16)
        send_p = jnp.where(valid, rows_p.reshape(-1)[entry], jnp.zeros((), jnp.bfloat16)).astype(jnp.bfloat16)
        return slot, send_x.reshape(EXPERTS, CAP, D), send_dy.reshape(EXPERTS, CAP, D), send_p.reshape(EXPERTS, CAP)

    def unpack(table, route_table, slot):
        rows = table[slot].astype(jnp.float32).reshape(TOK_DEV, TOP, D).sum(axis=1).astype(jnp.bfloat16)
        return rows, route_table[slot].reshape(TOK_DEV, TOP)

    def one_section(items):
        layer_x, layer_r, layer_p, layer_dy, wg, wu, wd = items
        slots, box_x, box_dy, box_p = jax.vmap(pack_source)(
            layer_x.reshape(N_EXPERT, TOK_DEV, D), layer_r.reshape(N_EXPERT, TOK_DEV, TOP),
            layer_p.reshape(N_EXPERT, TOK_DEV, TOP), layer_dy.reshape(N_EXPERT, TOK_DEV, D))
        box_x = box_x.transpose(1, 0, 2, 3).reshape(EXPERTS, N_EXPERT * CAP, D)
        box_dy = box_dy.transpose(1, 0, 2, 3).reshape(EXPERTS, N_EXPERT * CAP, D)
        box_p = box_p.transpose(1, 0, 2).reshape(EXPERTS, N_EXPERT * CAP)
        wg_each = wg.reshape(D, EXPERTS, FF).transpose(1, 0, 2)
        wu_each = wu.reshape(D, EXPERTS, FF).transpose(1, 0, 2)
        wd_each = wd.reshape(EXPERTS, FF, D)
        g_gate, g_up, g_down, part_dx, route_part = lax.map(expert_pass, (box_x, box_dy, box_p, wg_each, wu_each, wd_each))
        part_dx = part_dx.reshape(EXPERTS, N_EXPERT, CAP, D).transpose(1, 0, 2, 3).reshape(N_EXPERT, EXPERTS * CAP, D)
        route_part = route_part.reshape(EXPERTS, N_EXPERT, CAP).transpose(1, 0, 2).reshape(N_EXPERT, EXPERTS * CAP)
        layer_dx, layer_route = jax.vmap(unpack)(part_dx, route_part, slots)
        return (layer_dx.reshape(TOKENS, D), layer_route.reshape(TOKENS, TOP),
                g_gate.transpose(1, 0, 2).reshape(D, EXPERTS * FF),
                g_up.transpose(1, 0, 2).reshape(D, EXPERTS * FF),
                g_down.reshape(EXPERTS * FF, D))

    dx, route_grad, grad_gate, grad_up, grad_down = lax.map(one_section, (tokens, routes, probs, cotangent, w_gate, w_up, w_down))
    upstream = jnp.concatenate([dx[1:], jnp.zeros_like(dx[:1])], axis=0)
    return (upstream, route_grad, grad_gate, grad_up, grad_down)
```

```python
import jax
import jax.numpy as jnp
from jax import lax
from jax.experimental import pallas as pl
from jax.experimental.pallas import tpu as pltpu
from jax.sharding import PartitionSpec as P

BF = jnp.bfloat16
F32 = jnp.float32
SIDE = 4
EXPERTS = SIDE * SIDE
SLOTS = 32
TOK = 128
WIDTH = 2048
HALF = 384
TAIL = 128
CHUNK = 8
MESH = pl.DeviceIdType.MESH


def dot(a, b, dims):
    return lax.dot_general(a, b, (dims, ((), ())), preferred_element_type=F32)


def kernel(
    x_ref, routes_ref, probs_ref, dy_ref, wg_ref, wu_ref, wd_ref,
    up_ref, rg_ref, gg_ref, gu_ref, gd_ref,
    wgu, wdn, pair, metas, stage, rows, dab, hid, ret_out, ret_in, ggu, gdn,
    fin_out, fin_in, rfin_out, rfin_in,
    w_sem, z_send, z_recv, d_send, d_recv, r_send, r_recv, f_send, f_recv, l_sem, o_sem,
):
    sec = lax.axis_index("section")
    unit = lax.axis_index("expert")
    n_sec = lax.axis_size("section")
    zh = unit % 2
    ex = (unit // 2) % SIDE
    ey = unit // (2 * SIDE)
    mate = unit + 1 - 2 * zh
    prev = (sec + n_sec - 1) % n_sec

    def ahead(o):
        dx = o % SIDE
        dy = (o + o // SIDE) % SIDE
        return ((ey + dy) % SIDE * SIDE + (ex + dx) % SIDE) * 2 + zh

    def behind(o):
        dx = o % SIDE
        dy = (o + o // SIDE) % SIDE
        return ((ey + SIDE - dy) % SIDE * SIDE + (ex + SIDE - dx) % SIDE) * 2 + zh

    w_copies = [
        pltpu.make_async_copy(wg_ref, wgu.at[:, pl.ds(0, HALF)], w_sem.at[0]),
        pltpu.make_async_copy(wu_ref, wgu.at[:, pl.ds(HALF, HALF)], w_sem.at[1]),
        pltpu.make_async_copy(wd_ref, wdn, w_sem.at[2]),
    ]

    def to_mate(src, dst, i):
        return pltpu.make_async_remote_copy(
            src_ref=src, dst_ref=dst, send_sem=z_send.at[i], recv_sem=z_recv.at[i],
            device_id={"expert": mate}, device_id_type=MESH)

    z_copies = [
        to_mate(x_ref, pair.at[0], 0),
        to_mate(dy_ref, pair.at[1], 1),
        to_mate(metas.at[0], metas.at[1], 2),
    ]

    def dispatch(g, o):
        f = g * EXPERTS + o
        return pltpu.make_async_remote_copy(
            src_ref=stage.at[f], dst_ref=rows.at[f], send_sem=d_send.at[f], recv_sem=d_recv.at[f],
            device_id={"expert": ahead(o)}, device_id_type=MESH)

    def local_dispatch(g):
        f = g * EXPERTS
        return pltpu.make_async_copy(stage.at[f], rows.at[f], l_sem.at[g])

    def giveback(g, o):
        f = g * EXPERTS + o
        return pltpu.make_async_remote_copy(
            src_ref=ret_out.at[f], dst_ref=ret_in.at[f], send_sem=r_send.at[f], recv_sem=r_recv.at[f],
            device_id={"expert": behind(o)}, device_id_type=MESH)

    def local_giveback(g):
        f = g * EXPERTS
        return pltpu.make_async_copy(ret_out.at[f], ret_in.at[f], l_sem.at[g])

    def final(i):
        src, dst = ((fin_out.at[0], fin_in.at[0]), (fin_out.at[1], fin_in.at[1]), (rfin_out, rfin_in))[i]
        to = ({"section": prev}, {"section": prev, "expert": mate}, {"expert": mate})[i]
        return pltpu.make_async_remote_copy(
            src_ref=src, dst_ref=dst, send_sem=f_send.at[i], recv_sem=f_recv.at[i],
            device_id=to, device_id_type=MESH)

    z_copies[0].start()
    z_copies[1].start()
    for c in w_copies:
        c.start()

    lane = lax.broadcasted_iota(jnp.int32, (TOK, TOK), 1)
    row = lax.broadcasted_iota(jnp.int32, (TOK, TOK), 0)
    routes = routes_ref[...]
    probs = probs_ref[...].astype(F32)
    named = [routes[:, k : k + 1] for k in range(2)]
    member = ((named[0] == lane) | (named[1] == lane)).astype(BF)
    before = dot((lane < row).astype(BF), member, ((1,), (0,)))
    meta = jnp.zeros((TOK, TOK), F32)
    for k in range(2):
        place = jnp.sum(jnp.where(lane == named[k], before, 0.0), axis=1, keepdims=True)
        dx = (named[k] + (SIDE - ex)) % SIDE
        dy = (named[k] // SIDE + (SIDE - ey)) % SIDE
        order = dx + SIDE * ((dy + SIDE - dx) % SIDE)
        meta = jnp.where(lane == 2 * k, order.astype(F32), meta)
        meta = jnp.where(lane == 2 * k + 1, place, meta)
        meta = jnp.where(lane == 4 + k, probs[:, k : k + 1], meta)
    metas[0] = meta.astype(BF)
    z_copies[2].start()

    def picks(g):
        m = metas[g].astype(F32)
        slot_of = lax.broadcasted_iota(jnp.int32, (TOK, EXPERTS * SLOTS), 1)
        slots = [(m[:, 2 * k : 2 * k + 1] * SLOTS + m[:, 2 * k + 1 : 2 * k + 2]).astype(jnp.int32) for k in range(2)]
        return [slot_of == s for s in slots], [m[:, 4 + k : 5 + k] for k in range(2)]

    def pack(g, x_in, dy_in):
        hits, ps = picks(g)
        ones = (hits[0] | hits[1]).astype(BF)
        scaled = (jnp.where(hits[0], ps[0], 0.0) + jnp.where(hits[1], ps[1], 0.0)).astype(BF)
        for half in range(EXPERTS // CHUNK):
            cols = slice(half * CHUNK * SLOTS, (half + 1) * CHUNK * SLOTS)
            base = g * EXPERTS + half * CHUNK
            for which, (mat, src) in enumerate(((ones, x_in), (scaled, dy_in))):
                got = dot(mat[:, cols], src[...], ((0,), (0,))).astype(BF)
                stage[pl.ds(base, CHUNK), which] = got.reshape(CHUNK, SLOTS, WIDTH)
            if half == 0:
                local_dispatch(g).start()
            for o in range(half * CHUNK, (half + 1) * CHUNK):
                if o:
                    dispatch(g, o).start()

    pack(0, x_ref, dy_ref)
    for c in w_copies:
        c.wait()

    def work(i, _):
        g = i // (EXPERTS // CHUNK)
        first = (i % (EXPERTS // CHUNK)) * CHUNK

        @pl.when(i == 1)
        def _():
            for c in z_copies:
                c.wait_recv()
            pack(1, pair.at[0], pair.at[1])

        @pl.when(first == 0)
        def _():
            local_dispatch(g).wait()

        def arrive(j, _):
            o = first + j

            @pl.when(o > 0)
            def _():
                dispatch(g, o).wait_recv()

            return 0

        lax.fori_loop(0, CHUNK, arrive, 0)
        f = pl.multiple_of(i * CHUNK, CHUNK)
        r = pl.multiple_of(i * CHUNK * SLOTS, CHUNK * SLOTS)
        n = CHUNK * SLOTS
        x = rows[pl.ds(f, CHUNK), 0].reshape(n, WIDTH)
        dyp = rows[pl.ds(f, CHUNK), 1].reshape(n, WIDTH)
        ab = dot(x, wgu[...], ((1,), (0,)))
        q = dot(dyp, wdn[...], ((1,), (1,)))
        a, b = ab[:, :HALF], ab[:, HALF:]
        sig = jax.nn.sigmoid(a)
        act = a * sig
        h = (act * b).astype(BF)
        part = jnp.sum(q * h.astype(F32), axis=1, keepdims=True)
        d_gate = (q * b * sig * (1.0 + a * (1.0 - sig))).astype(BF)
        d_up = (q * act).astype(BF)
        hid[pl.ds(r, n), :] = h
        dab[pl.ds(r, n), pl.ds(0, HALF)] = d_gate
        dab[pl.ds(r, n), pl.ds(HALF, HALF)] = d_up
        both = dab[pl.ds(r, n), :]
        back = dot(both, wgu[...], ((1,), (1,))).astype(BF)
        ret_out[pl.ds(f, CHUNK), :, pl.ds(0, WIDTH)] = back.reshape(CHUNK, SLOTS, WIDTH)
        high = part.astype(BF).astype(F32)
        at = lax.broadcasted_iota(jnp.int32, (n, TAIL), 1)
        tail = jnp.where(at == 0, high, jnp.where(at == 1, part - high, 0.0)).astype(BF)
        ret_out[pl.ds(f, CHUNK), :, pl.ds(WIDTH, TAIL)] = tail.reshape(CHUNK, SLOTS, TAIL)

        @pl.when(first == 0)
        def _():
            local_giveback(g).start()

        def leave(j, _):
            o = first + j

            @pl.when(o > 0)
            def _():
                giveback(g, o).start()

            return 0

        lax.fori_loop(0, CHUNK, leave, 0)
        return 0

    lax.fori_loop(0, 2 * EXPERTS // CHUNK, work, 0)

    n_rows = 2 * EXPERTS * SLOTS
    tile = 256

    def grads(t, _):
        cols = pl.ds(pl.multiple_of(t * tile, tile), tile)
        xt = rows[:, 0, :, cols].reshape(n_rows, tile)
        ggu[cols, :] = dot(xt, dab[...], ((0,), (0,))).astype(BF)
        dyt = rows[:, 1, :, cols].reshape(n_rows, tile)
        gdn[:, cols] = dot(hid[...], dyt, ((0,), (0,))).astype(BF)
        return 0

    lax.fori_loop(0, WIDTH // tile, grads, 0)
    o_copies = [
        pltpu.make_async_copy(ggu.at[:, pl.ds(0, HALF)], gg_ref, o_sem.at[0]),
        pltpu.make_async_copy(ggu.at[:, pl.ds(HALF, HALF)], gu_ref, o_sem.at[1]),
        pltpu.make_async_copy(gdn, gd_ref, o_sem.at[2]),
    ]
    for c in o_copies:
        c.start()

    def join(g):
        local_giveback(g).wait()

        def arrive(o, _):
            giveback(g, o).wait_recv()
            return 0

        lax.fori_loop(1, EXPERTS, arrive, 0)
        hits, _ = picks(g)
        got = ret_in.at[pl.ds(g * EXPERTS, EXPERTS)]
        mine = (hits[0] | hits[1]).astype(BF)
        dx = dot(mine, got[:, :, pl.ds(0, WIDTH)].reshape(EXPERTS * SLOTS, WIDTH), ((1,), (0,)))
        fin_out[g] = dx.astype(BF)
        final(g).start()
        tail = got[:, :, pl.ds(WIDTH, TAIL)].reshape(EXPERTS * SLOTS, TAIL)
        parts = [dot(hits[k].astype(BF), tail, ((1,), (0,))) for k in range(2)]
        return [v[:, 0:1] + v[:, 1:2] for v in parts]

    own = join(0)
    other = join(1)
    rfin_out[...] = jnp.where(lane == 0, other[0], jnp.where(lane == 1, other[1], 0.0))
    final(2).start()

    final(2).wait_recv()
    there = rfin_in[...]
    total = [(own[k] + there[:, k : k + 1]) / probs[:, k : k + 1] for k in range(2)]
    pairs = jnp.where(lane == 0, total[0], jnp.where(lane == 1, total[1], 0.0))
    rg_ref[...] = pairs[:, :2].astype(BF)
    final(0).wait_recv()
    final(1).wait_recv()
    summed = fin_in[0].astype(F32) + fin_in[1].astype(F32)
    up_ref[...] = jnp.where(sec == n_sec - 1, 0.0, summed).astype(BF)

    for c in z_copies:
        c.wait_send()
    for i in range(3):
        final(i).wait_send()

    def left(o, _):
        for g in range(2):
            dispatch(g, o).wait_send()
            giveback(g, o).wait_send()
        return 0

    lax.fori_loop(1, EXPERTS, left, 0)
    for c in o_copies:
        c.wait()


def body(tokens, routes, probs, cotangent, w_gate, w_up, w_down):
    vmem = pl.BlockSpec(memory_space=pltpu.VMEM)
    hbm = pl.BlockSpec(memory_space=pl.ANY)
    blocks = 2 * EXPERTS
    n_rows = blocks * SLOTS
    out = pl.pallas_call(
        kernel,
        out_shape=(
            jax.ShapeDtypeStruct((TOK, WIDTH), BF),
            jax.ShapeDtypeStruct((TOK, 2), BF),
            jax.ShapeDtypeStruct((WIDTH, HALF), BF),
            jax.ShapeDtypeStruct((WIDTH, HALF), BF),
            jax.ShapeDtypeStruct((HALF, WIDTH), BF),
        ),
        in_specs=[vmem, vmem, vmem, vmem, hbm, hbm, hbm],
        out_specs=(vmem, vmem, hbm, hbm, hbm),
        scratch_shapes=[
            pltpu.VMEM((WIDTH, 2 * HALF), BF),
            pltpu.VMEM((HALF, WIDTH), BF),
            pltpu.VMEM((2, TOK, WIDTH), BF),
            pltpu.VMEM((2, TOK, TOK), BF),
            pltpu.VMEM((blocks, 2, SLOTS, WIDTH), BF),
            pltpu.VMEM((blocks, 2, SLOTS, WIDTH), BF),
            pltpu.VMEM((n_rows, 2 * HALF), BF),
            pltpu.VMEM((n_rows, HALF), BF),
            pltpu.VMEM((blocks, SLOTS, WIDTH + TAIL), BF),
            pltpu.VMEM((blocks, SLOTS, WIDTH + TAIL), BF),
            pltpu.VMEM((WIDTH, 2 * HALF), BF),
            pltpu.VMEM((HALF, WIDTH), BF),
            pltpu.VMEM((2, TOK, WIDTH), BF),
            pltpu.VMEM((2, TOK, WIDTH), BF),
            pltpu.VMEM((TOK, TOK), F32),
            pltpu.VMEM((TOK, TOK), F32),
            pltpu.SemaphoreType.DMA((3,)),
            pltpu.SemaphoreType.DMA((3,)),
            pltpu.SemaphoreType.DMA((3,)),
            pltpu.SemaphoreType.DMA((blocks,)),
            pltpu.SemaphoreType.DMA((blocks,)),
            pltpu.SemaphoreType.DMA((blocks,)),
            pltpu.SemaphoreType.DMA((blocks,)),
            pltpu.SemaphoreType.DMA((3,)),
            pltpu.SemaphoreType.DMA((3,)),
            pltpu.SemaphoreType.DMA((2,)),
            pltpu.SemaphoreType.DMA((3,)),
        ],
        compiler_params=pltpu.CompilerParams(has_side_effects=True, vmem_limit_bytes=58 << 20),
        name="expert_backward",
    )(tokens[0], routes[0], probs[0], cotangent[0], w_gate[0], w_up[0], w_down[0])
    return tuple(o[None] for o in out)


def solution(mesh):
    by_token = P("section", "expert", None)
    by_column = P("section", None, "expert")
    return jax.shard_map(
        body,
        mesh=mesh,
        in_specs=(by_token, by_token, by_token, by_token, by_column, by_column, by_token),
        out_specs=(by_token, by_token, by_column, by_column, by_token),
        check_vma=False,
    )
```

```python
import jax
import jax.numpy as jnp
from jax import lax
from jax.experimental import pallas as pl
from jax.experimental.pallas import tpu as pltpu
from jax.sharding import PartitionSpec as P

BF = jnp.bfloat16
F32 = jnp.float32
SIDE = 4
EXPERTS = SIDE * SIDE
SLOTS = 32
TOK = 128
WIDTH = 2048
HALF = 384
TAIL = 128
CHUNK = 8
REST = 512
MAIN = WIDTH - REST
EARLY = 12
MESH = pl.DeviceIdType.MESH


def dot(a, b, dims):
    return lax.dot_general(a, b, (dims, ((), ())), preferred_element_type=F32)


def kernel(
    x_ref, routes_ref, probs_ref, dy_ref, wg_ref, wu_ref, wd_ref,
    up_ref, rg_ref, gg_ref, gu_ref, gd_ref,
    wgu, wdn, pair, metas, stage, stage_b, rows, rows_b, dab, hid, ret_out, ret_in, ggu, gdn,
    fin_out, fin_in, rfin_out, rfin_in,
    w_sem, z_send, z_recv, d_send, d_recv, b_send, b_recv, c_send, c_recv, r_send, r_recv, f_send, f_recv, l_sem, o_sem,
):
    sec = lax.axis_index("section")
    unit = lax.axis_index("expert")
    n_sec = lax.axis_size("section")
    zh = unit % 2
    ex = (unit // 2) % SIDE
    ey = unit // (2 * SIDE)
    mate = unit + 1 - 2 * zh
    prev = (sec + n_sec - 1) % n_sec

    def ahead(o):
        dx = o % SIDE
        dy = (o + o // SIDE) % SIDE
        return ((ey + dy) % SIDE * SIDE + (ex + dx) % SIDE) * 2 + zh

    def behind(o):
        dx = o % SIDE
        dy = (o + o // SIDE) % SIDE
        return ((ey + SIDE - dy) % SIDE * SIDE + (ex + SIDE - dx) % SIDE) * 2 + zh

    w_copies = [
        pltpu.make_async_copy(wg_ref, wgu.at[:, pl.ds(0, HALF)], w_sem.at[0]),
        pltpu.make_async_copy(wu_ref, wgu.at[:, pl.ds(HALF, HALF)], w_sem.at[1]),
        pltpu.make_async_copy(wd_ref, wdn, w_sem.at[2]),
    ]

    def to_mate(src, dst, i):
        return pltpu.make_async_remote_copy(
            src_ref=src, dst_ref=dst, send_sem=z_send.at[i], recv_sem=z_recv.at[i],
            device_id={"expert": mate}, device_id_type=MESH)

    z_copies = [
        to_mate(x_ref.at[:, pl.ds(0, MAIN)], pair.at[0], 0),
        to_mate(dy_ref.at[:, pl.ds(0, MAIN)], pair.at[1], 1),
        to_mate(metas.at[0], metas.at[1], 2),
    ]

    def dispatch(g, o):
        f = g * EXPERTS + o
        return pltpu.make_async_remote_copy(
            src_ref=stage.at[f], dst_ref=rows.at[f], send_sem=d_send.at[f], recv_sem=d_recv.at[f],
            device_id={"expert": ahead(o)}, device_id_type=MESH)

    def dispatch_rest(o):
        return pltpu.make_async_remote_copy(
            src_ref=stage_b.at[o], dst_ref=rows_b.at[o], send_sem=b_send.at[o], recv_sem=b_recv.at[o],
            device_id={"expert": ahead(o)}, device_id_type=MESH)

    def across(o):
        return pltpu.make_async_remote_copy(
            src_ref=rows_b.at[o], dst_ref=rows_b.at[EXPERTS + o], send_sem=c_send.at[o], recv_sem=c_recv.at[o],
            device_id={"expert": mate}, device_id_type=MESH)

    def giveback(g, o):
        f = g * EXPERTS + o
        return pltpu.make_async_remote_copy(
            src_ref=ret_out.at[f], dst_ref=ret_in.at[f], send_sem=r_send.at[f], recv_sem=r_recv.at[f],
            device_id={"expert": behind(o)}, device_id_type=MESH)

    def local_giveback(g):
        f = g * EXPERTS
        return pltpu.make_async_copy(ret_out.at[f], ret_in.at[f], l_sem.at[g])

    def final(i):
        src, dst = ((fin_out.at[0], fin_in.at[0]), (fin_out.at[1], fin_in.at[1]), (rfin_out, rfin_in))[i]
        to = ({"section": prev}, {"section": prev, "expert": mate}, {"expert": mate})[i]
        return pltpu.make_async_remote_copy(
            src_ref=src, dst_ref=dst, send_sem=f_send.at[i], recv_sem=f_recv.at[i],
            device_id=to, device_id_type=MESH)

    z_copies[0].start()
    z_copies[1].start()
    for c in w_copies:
        c.start()

    lane = lax.broadcasted_iota(jnp.int32, (TOK, TOK), 1)
    row = lax.broadcasted_iota(jnp.int32, (TOK, TOK), 0)
    diagonal = row == lane

    def column(v):
        return jnp.sum(jnp.where(diagonal, v, 0.0), axis=1, keepdims=True)

    routes = routes_ref[...].astype(F32)
    chances = probs_ref[...].astype(F32)
    named = [column(routes[k : k + 1, :]).astype(jnp.int32) for k in range(2)]
    probs = [column(chances[k : k + 1, :]) for k in range(2)]
    member = ((named[0] == lane) | (named[1] == lane)).astype(BF)
    before = dot((lane < row).astype(BF), member, ((1,), (0,)))
    meta = jnp.zeros((TOK, TOK), F32)
    for k in range(2):
        place = jnp.sum(jnp.where(lane == named[k], before, 0.0), axis=1, keepdims=True)
        dx = (named[k] + (SIDE - ex)) % SIDE
        dy = (named[k] // SIDE + (SIDE - ey)) % SIDE
        order = dx + SIDE * ((dy + SIDE - dx) % SIDE)
        meta = jnp.where(lane == 2 * k, order.astype(F32), meta)
        meta = jnp.where(lane == 2 * k + 1, place, meta)
        meta = jnp.where(lane == 4 + k, probs[k], meta)
    metas[0] = meta.astype(BF)
    z_copies[2].start()

    def picks(g):
        m = metas[g].astype(F32)
        slot_of = lax.broadcasted_iota(jnp.int32, (TOK, EXPERTS * SLOTS), 1)
        slots = [(m[:, 2 * k : 2 * k + 1] * SLOTS + m[:, 2 * k + 1 : 2 * k + 2]).astype(jnp.int32) for k in range(2)]
        return [slot_of == s for s in slots], [m[:, 4 + k : 5 + k] for k in range(2)]

    def masks(g):
        hits, ps = picks(g)
        ones = (hits[0] | hits[1]).astype(BF)
        scaled = (jnp.where(hits[0], ps[0], 0.0) + jnp.where(hits[1], ps[1], 0.0)).astype(BF)
        return ones, scaled

    def pack(g, half, mats, srcs, cols, out, arrived):
        take = slice(half * CHUNK * SLOTS, (half + 1) * CHUNK * SLOTS)
        base = g * EXPERTS + half * CHUNK
        for which, (mat, src) in enumerate(zip(mats, srcs)):
            got = dot(mat[:, take], src[:, cols], ((0,), (0,))).astype(BF)
            got = got.reshape(CHUNK, SLOTS, got.shape[1])
            out[pl.ds(base, CHUNK), which] = got
            if half == 0:
                arrived[base, which] = got[0]

    def send(g, lo, hi):
        for o in range(max(lo, 1), hi):
            dispatch(g, o).start()

    own_masks = masks(0)
    for half in range(EXPERTS // CHUNK):
        pack(0, half, own_masks, (x_ref, dy_ref), pl.ds(MAIN, REST), stage_b, rows_b)
        if half == 0:
            across(0).start()
        for o in range(max(half * CHUNK, 1), (half + 1) * CHUNK):
            dispatch_rest(o).start()
    pack(0, 0, own_masks, (x_ref, dy_ref), pl.ds(0, MAIN), stage, rows)
    send(0, 0, CHUNK)
    pack(0, 1, own_masks, (x_ref, dy_ref), pl.ds(0, MAIN), stage, rows)
    send(0, CHUNK, EARLY)

    def pass_on(o, _):
        dispatch_rest(o).wait_recv()
        across(o).start()
        return 0

    lax.fori_loop(1, EXPERTS, pass_on, 0)
    for c in z_copies:
        c.wait_recv()
    mate_masks = masks(1)
    for half in range(EXPERTS // CHUNK):
        pack(1, half, mate_masks, (pair.at[0], pair.at[1]), pl.ds(0, MAIN), stage, rows)
        send(1, half * CHUNK, (half + 1) * CHUNK)
    send(0, EARLY, EXPERTS)
    for c in w_copies:
        c.wait()

    def work(i, _):
        g = (i + 1) // 2 % 2
        first = i // 2 * CHUNK

        def arrive(j, _):
            o = first + j

            @pl.when(o > 0)
            def _():
                dispatch(g, o).wait_recv()

            @pl.when(g == 1)
            def _():
                across(o).wait_recv()

            return 0

        lax.fori_loop(0, CHUNK, arrive, 0)
        f = pl.multiple_of(g * EXPERTS + first, CHUNK)
        r = pl.multiple_of(f * SLOTS, CHUNK * SLOTS)
        n = CHUNK * SLOTS
        x = rows[pl.ds(f, CHUNK), 0].reshape(n, MAIN)
        dyp = rows[pl.ds(f, CHUNK), 1].reshape(n, MAIN)
        x_b = rows_b[pl.ds(f, CHUNK), 0].reshape(n, REST)
        dyp_b = rows_b[pl.ds(f, CHUNK), 1].reshape(n, REST)
        ab = dot(x, wgu[pl.ds(0, MAIN), :], ((1,), (0,))) + dot(x_b, wgu[pl.ds(MAIN, REST), :], ((1,), (0,)))
        q = dot(dyp, wdn[:, pl.ds(0, MAIN)], ((1,), (1,))) + dot(dyp_b, wdn[:, pl.ds(MAIN, REST)], ((1,), (1,)))
        a, b = ab[:, :HALF], ab[:, HALF:]
        sig = jax.nn.sigmoid(a)
        act = a * sig
        h = (act * b).astype(BF)
        part = jnp.sum(q * h.astype(F32), axis=1, keepdims=True)
        d_gate = (q * b * sig * (1.0 + a * (1.0 - sig))).astype(BF)
        d_up = (q * act).astype(BF)
        hid[pl.ds(r, n), :] = h
        dab[pl.ds(r, n), pl.ds(0, HALF)] = d_gate
        dab[pl.ds(r, n), pl.ds(HALF, HALF)] = d_up
        both = dab[pl.ds(r, n), :]
        back = dot(both, wgu[...], ((1,), (1,))).astype(BF)
        ret_out[pl.ds(f, CHUNK), :, pl.ds(0, WIDTH)] = back.reshape(CHUNK, SLOTS, WIDTH)
        high = part.astype(BF).astype(F32)
        at = lax.broadcasted_iota(jnp.int32, (n, TAIL), 1)
        tail = jnp.where(at == 0, high, jnp.where(at == 1, part - high, 0.0)).astype(BF)
        ret_out[pl.ds(f, CHUNK), :, pl.ds(WIDTH, TAIL)] = tail.reshape(CHUNK, SLOTS, TAIL)

        @pl.when(first == 0)
        def _():
            local_giveback(g).start()

        def leave(j, _):
            o = first + j

            @pl.when(o > 0)
            def _():
                giveback(g, o).start()

            return 0

        lax.fori_loop(0, CHUNK, leave, 0)
        return 0

    lax.fori_loop(0, 2 * EXPERTS // CHUNK, work, 0)

    def join(g):
        local_giveback(g).wait()

        def arrive(o, _):
            giveback(g, o).wait_recv()
            return 0

        lax.fori_loop(1, EXPERTS, arrive, 0)
        hits, _ = picks(g)
        got = ret_in.at[pl.ds(g * EXPERTS, EXPERTS)]
        mine = (hits[0] | hits[1]).astype(BF)
        dx = dot(mine, got[:, :, pl.ds(0, WIDTH)].reshape(EXPERTS * SLOTS, WIDTH), ((1,), (0,)))
        fin_out[g] = dx.astype(BF)
        final(g).start()
        tail = got[:, :, pl.ds(WIDTH, TAIL)].reshape(EXPERTS * SLOTS, TAIL)
        parts = [dot(hits[k].astype(BF), tail, ((1,), (0,))) for k in range(2)]
        return [v[:, 0:1] + v[:, 1:2] for v in parts]

    other = join(1)
    rfin_out[...] = jnp.where(lane == 0, other[0], jnp.where(lane == 1, other[1], 0.0))
    final(2).start()

    n_rows = 2 * EXPERTS * SLOTS
    tile = 256

    def grads(held, start):
        def one(t, _):
            cols = pl.ds(pl.multiple_of(t * tile, tile), tile)
            to = pl.ds(pl.multiple_of(start + t * tile, tile), tile)
            xt = held[:, 0, :, cols].reshape(n_rows, tile)
            ggu[to, :] = dot(xt, dab[...], ((0,), (0,))).astype(BF)
            dyt = held[:, 1, :, cols].reshape(n_rows, tile)
            gdn[:, to] = dot(hid[...], dyt, ((0,), (0,))).astype(BF)
            return 0

        lax.fori_loop(0, held.shape[3] // tile, one, 0)

    grads(rows, 0)
    grads(rows_b, MAIN)
    o_copies = [
        pltpu.make_async_copy(ggu.at[:, pl.ds(0, HALF)], gg_ref, o_sem.at[0]),
        pltpu.make_async_copy(ggu.at[:, pl.ds(HALF, HALF)], gu_ref, o_sem.at[1]),
        pltpu.make_async_copy(gdn, gd_ref, o_sem.at[2]),
    ]
    for c in o_copies:
        c.start()

    own = join(0)
    final(2).wait_recv()
    there = rfin_in[...]
    total = [(own[k] + there[:, k : k + 1]) / probs[k] for k in range(2)]
    lines = [jnp.sum(jnp.where(diagonal, v, 0.0), axis=0, keepdims=True) for v in total]
    which = lax.broadcasted_iota(jnp.int32, (2, TOK), 0)
    rg_ref[...] = jnp.where(which == 0, lines[0], lines[1]).astype(BF)
    final(0).wait_recv()
    final(1).wait_recv()
    summed = fin_in[0].astype(F32) + fin_in[1].astype(F32)
    up_ref[...] = jnp.where(sec == n_sec - 1, 0.0, summed).astype(BF)

    for c in z_copies:
        c.wait_send()
    for i in range(3):
        final(i).wait_send()

    def left(o, _):
        for g in range(2):
            dispatch(g, o).wait_send()
            giveback(g, o).wait_send()
        dispatch_rest(o).wait_send()
        across(o).wait_send()
        return 0

    across(0).wait_send()
    lax.fori_loop(1, EXPERTS, left, 0)
    for c in o_copies:
        c.wait()


def body(tokens, routes, probs, cotangent, w_gate, w_up, w_down):
    vmem = pl.BlockSpec(memory_space=pltpu.VMEM)
    hbm = pl.BlockSpec(memory_space=pl.ANY)
    blocks = 2 * EXPERTS
    n_rows = blocks * SLOTS
    out = pl.pallas_call(
        kernel,
        out_shape=(
            jax.ShapeDtypeStruct((TOK, WIDTH), BF),
            jax.ShapeDtypeStruct((2, TOK), BF),
            jax.ShapeDtypeStruct((WIDTH, HALF), BF),
            jax.ShapeDtypeStruct((WIDTH, HALF), BF),
            jax.ShapeDtypeStruct((HALF, WIDTH), BF),
        ),
        in_specs=[vmem, vmem, vmem, vmem, hbm, hbm, hbm],
        out_specs=(vmem, vmem, hbm, hbm, hbm),
        scratch_shapes=[
            pltpu.VMEM((WIDTH, 2 * HALF), BF),
            pltpu.VMEM((HALF, WIDTH), BF),
            pltpu.VMEM((2, TOK, MAIN), BF),
            pltpu.VMEM((2, TOK, TOK), BF),
            pltpu.VMEM((blocks, 2, SLOTS, MAIN), BF),
            pltpu.VMEM((EXPERTS, 2, SLOTS, REST), BF),
            pltpu.VMEM((blocks, 2, SLOTS, MAIN), BF),
            pltpu.VMEM((blocks, 2, SLOTS, REST), BF),
            pltpu.VMEM((n_rows, 2 * HALF), BF),
            pltpu.VMEM((n_rows, HALF), BF),
            pltpu.VMEM((blocks, SLOTS, WIDTH + TAIL), BF),
            pltpu.VMEM((blocks, SLOTS, WIDTH + TAIL), BF),
            pltpu.VMEM((WIDTH, 2 * HALF), BF),
            pltpu.VMEM((HALF, WIDTH), BF),
            pltpu.VMEM((2, TOK, WIDTH), BF),
            pltpu.VMEM((2, TOK, WIDTH), BF),
            pltpu.VMEM((TOK, TOK), F32),
            pltpu.VMEM((TOK, TOK), F32),
            pltpu.SemaphoreType.DMA((3,)),
            pltpu.SemaphoreType.DMA((3,)),
            pltpu.SemaphoreType.DMA((3,)),
            pltpu.SemaphoreType.DMA((blocks,)),
            pltpu.SemaphoreType.DMA((blocks,)),
            pltpu.SemaphoreType.DMA((EXPERTS,)),
            pltpu.SemaphoreType.DMA((EXPERTS,)),
            pltpu.SemaphoreType.DMA((EXPERTS,)),
            pltpu.SemaphoreType.DMA((EXPERTS,)),
            pltpu.SemaphoreType.DMA((blocks,)),
            pltpu.SemaphoreType.DMA((blocks,)),
            pltpu.SemaphoreType.DMA((3,)),
            pltpu.SemaphoreType.DMA((3,)),
            pltpu.SemaphoreType.DMA((2,)),
            pltpu.SemaphoreType.DMA((3,)),
        ],
        compiler_params=pltpu.CompilerParams(has_side_effects=True, vmem_limit_bytes=58 << 20),
        name="expert_backward",
    )(tokens[0], routes[0].T, probs[0].T, cotangent[0], w_gate[0], w_up[0], w_down[0])
    upstream, route_grad, g_gate, g_up, g_down = out
    return upstream[None], route_grad.T[None], g_gate[None], g_up[None], g_down[None]


def solution(mesh):
    by_token = P("section", "expert", None)
    by_column = P("section", None, "expert")
    return jax.shard_map(
        body,
        mesh=mesh,
        in_specs=(by_token, by_token, by_token, by_token, by_column, by_column, by_token),
        out_specs=(by_token, by_token, by_column, by_column, by_token),
        check_vma=False,
    )
```

```python
import jax
import jax.numpy as jnp
from jax import lax
from jax.experimental import pallas as pl
from jax.experimental.pallas import tpu as pltpu
from jax.sharding import PartitionSpec as P

BF = jnp.bfloat16
F32 = jnp.float32
SIDE = 4
EXPERTS = SIDE * SIDE
SLOTS = 32
TOK = 128
WIDTH = 2048
HALF = 384
TAIL = 128
CHUNK = 8
REST = 768
MAIN = WIDTH - REST
EARLY = 12
MESH = pl.DeviceIdType.MESH


def dot(a, b, dims):
    return lax.dot_general(a, b, (dims, ((), ())), preferred_element_type=F32)


def kernel(
    x_ref, routes_ref, probs_ref, dy_ref, wg_ref, wu_ref, wd_ref,
    up_ref, rg_ref, gg_ref, gu_ref, gd_ref,
    wgu, wdn, pair, metas, stage, stage_b, rows, rows_b, dab, hid, ret_out, ret_in, ggu, gdn,
    fin_out, fin_in, rfin_out, rfin_in,
    w_sem, z_send, z_recv, d_send, d_recv, b_send, b_recv, c_send, c_recv, r_send, r_recv, f_send, f_recv, l_sem, o_sem,
):
    sec = lax.axis_index("section")
    unit = lax.axis_index("expert")
    n_sec = lax.axis_size("section")
    zh = unit % 2
    ex = (unit // 2) % SIDE
    ey = unit // (2 * SIDE)
    mate = unit + 1 - 2 * zh
    prev = (sec + n_sec - 1) % n_sec

    def ahead(o):
        dx = o % SIDE
        dy = (o + o // SIDE) % SIDE
        return ((ey + dy) % SIDE * SIDE + (ex + dx) % SIDE) * 2 + zh

    def behind(o):
        dx = o % SIDE
        dy = (o + o // SIDE) % SIDE
        return ((ey + SIDE - dy) % SIDE * SIDE + (ex + SIDE - dx) % SIDE) * 2 + zh

    w_copies = [
        pltpu.make_async_copy(wg_ref, wgu.at[:, pl.ds(0, HALF)], w_sem.at[0]),
        pltpu.make_async_copy(wu_ref, wgu.at[:, pl.ds(HALF, HALF)], w_sem.at[1]),
        pltpu.make_async_copy(wd_ref, wdn, w_sem.at[2]),
    ]

    def to_mate(src, dst, i):
        return pltpu.make_async_remote_copy(
            src_ref=src, dst_ref=dst, send_sem=z_send.at[i], recv_sem=z_recv.at[i],
            device_id={"expert": mate}, device_id_type=MESH)

    z_copies = [
        to_mate(x_ref.at[:, pl.ds(0, MAIN)], pair.at[0], 0),
        to_mate(dy_ref.at[:, pl.ds(0, MAIN)], pair.at[1], 1),
        to_mate(metas.at[0], metas.at[1], 2),
    ]

    def dispatch(g, o):
        f = g * EXPERTS + o
        return pltpu.make_async_remote_copy(
            src_ref=stage.at[f], dst_ref=rows.at[f], send_sem=d_send.at[f], recv_sem=d_recv.at[f],
            device_id={"expert": ahead(o)}, device_id_type=MESH)

    def dispatch_rest(o):
        return pltpu.make_async_remote_copy(
            src_ref=stage_b.at[o], dst_ref=rows_b.at[o], send_sem=b_send.at[o], recv_sem=b_recv.at[o],
            device_id={"expert": ahead(o)}, device_id_type=MESH)

    def across(o):
        return pltpu.make_async_remote_copy(
            src_ref=rows_b.at[o], dst_ref=rows_b.at[EXPERTS + o], send_sem=c_send.at[o], recv_sem=c_recv.at[o],
            device_id={"expert": mate}, device_id_type=MESH)

    def giveback(g, o):
        f = g * EXPERTS + o
        return pltpu.make_async_remote_copy(
            src_ref=ret_out.at[f], dst_ref=ret_in.at[f], send_sem=r_send.at[f], recv_sem=r_recv.at[f],
            device_id={"expert": behind(o)}, device_id_type=MESH)

    def local_giveback(g):
        f = g * EXPERTS
        return pltpu.make_async_copy(ret_out.at[f], ret_in.at[f], l_sem.at[g])

    def final(i):
        src, dst = ((fin_out.at[0], fin_in.at[0]), (fin_out.at[1], fin_in.at[1]), (rfin_out, rfin_in))[i]
        to = ({"section": prev}, {"section": prev, "expert": mate}, {"expert": mate})[i]
        return pltpu.make_async_remote_copy(
            src_ref=src, dst_ref=dst, send_sem=f_send.at[i], recv_sem=f_recv.at[i],
            device_id=to, device_id_type=MESH)

    following = (sec + 1) % n_sec
    gate = pltpu.get_barrier_semaphore()
    others = [{"expert": ahead(o)} for o in range(1, EXPERTS)] + [{"expert": mate}]
    others += [{"section": s, "expert": u} for s in (prev, following) for u in (unit, mate)]
    for other in others:
        pl.semaphore_signal(gate, inc=1, device_id=other, device_id_type=MESH)
    pl.semaphore_wait(gate, len(others))

    z_copies[0].start()
    z_copies[1].start()
    for c in w_copies:
        c.start()

    lane = lax.broadcasted_iota(jnp.int32, (TOK, TOK), 1)
    row = lax.broadcasted_iota(jnp.int32, (TOK, TOK), 0)
    diagonal = row == lane

    def column(v):
        return jnp.sum(jnp.where(diagonal, v, 0.0), axis=1, keepdims=True)

    routes = routes_ref[...].astype(F32)
    chances = probs_ref[...].astype(F32)
    named = [column(routes[k : k + 1, :]).astype(jnp.int32) for k in range(2)]
    probs = [column(chances[k : k + 1, :]) for k in range(2)]
    member = ((named[0] == lane) | (named[1] == lane)).astype(BF)
    before = dot((lane < row).astype(BF), member, ((1,), (0,)))
    meta = jnp.zeros((TOK, TOK), F32)
    for k in range(2):
        place = jnp.sum(jnp.where(lane == named[k], before, 0.0), axis=1, keepdims=True)
        dx = (named[k] + (SIDE - ex)) % SIDE
        dy = (named[k] // SIDE + (SIDE - ey)) % SIDE
        order = dx + SIDE * ((dy + SIDE - dx) % SIDE)
        meta = jnp.where(lane == 2 * k, order.astype(F32), meta)
        meta = jnp.where(lane == 2 * k + 1, place, meta)
        meta = jnp.where(lane == 4 + k, probs[k], meta)
    metas[0] = meta.astype(BF)
    z_copies[2].start()

    def picks(g):
        m = metas[g].astype(F32)
        slot_of = lax.broadcasted_iota(jnp.int32, (TOK, EXPERTS * SLOTS), 1)
        slots = [(m[:, 2 * k : 2 * k + 1] * SLOTS + m[:, 2 * k + 1 : 2 * k + 2]).astype(jnp.int32) for k in range(2)]
        return [slot_of == s for s in slots], [m[:, 4 + k : 5 + k] for k in range(2)]

    def masks(g):
        hits, ps = picks(g)
        ones = (hits[0] | hits[1]).astype(BF)
        scaled = (jnp.where(hits[0], ps[0], 0.0) + jnp.where(hits[1], ps[1], 0.0)).astype(BF)
        return ones, scaled

    def pack(g, half, mats, srcs, cols, out, arrived):
        take = slice(half * CHUNK * SLOTS, (half + 1) * CHUNK * SLOTS)
        base = g * EXPERTS + half * CHUNK
        for which, (mat, src) in enumerate(zip(mats, srcs)):
            got = dot(mat[:, take], src[:, cols], ((0,), (0,))).astype(BF)
            got = got.reshape(CHUNK, SLOTS, got.shape[1])
            out[pl.ds(base, CHUNK), which] = got
            if half == 0:
                arrived[base, which] = got[0]

    def send(g, lo, hi):
        for o in range(max(lo, 1), hi):
            dispatch(g, o).start()

    own_masks = masks(0)
    for half in range(EXPERTS // CHUNK):
        pack(0, half, own_masks, (x_ref, dy_ref), pl.ds(MAIN, REST), stage_b, rows_b)
        if half == 0:
            across(0).start()
        for o in range(max(half * CHUNK, 1), (half + 1) * CHUNK):
            dispatch_rest(o).start()
    pack(0, 0, own_masks, (x_ref, dy_ref), pl.ds(0, MAIN), stage, rows)
    send(0, 0, CHUNK)
    pack(0, 1, own_masks, (x_ref, dy_ref), pl.ds(0, MAIN), stage, rows)
    send(0, CHUNK, EARLY)

    def pass_on(o, _):
        dispatch_rest(o).wait_recv()
        across(o).start()
        return 0

    lax.fori_loop(1, EXPERTS, pass_on, 0)
    for c in z_copies:
        c.wait_recv()
    mate_masks = masks(1)
    for half in range(EXPERTS // CHUNK):
        pack(1, half, mate_masks, (pair.at[0], pair.at[1]), pl.ds(0, MAIN), stage, rows)
        send(1, half * CHUNK, (half + 1) * CHUNK)
    send(0, EARLY, EXPERTS)
    for c in w_copies:
        c.wait()

    def work(i, _):
        g = (i + 1) // 2 % 2
        first = i // 2 * CHUNK

        def arrive(j, _):
            o = first + j

            @pl.when(o > 0)
            def _():
                dispatch(g, o).wait_recv()

            @pl.when(g == 1)
            def _():
                across(o).wait_recv()

            return 0

        lax.fori_loop(0, CHUNK, arrive, 0)
        f = pl.multiple_of(g * EXPERTS + first, CHUNK)
        r = pl.multiple_of(f * SLOTS, CHUNK * SLOTS)
        n = CHUNK * SLOTS
        x = rows[pl.ds(f, CHUNK), 0].reshape(n, MAIN)
        dyp = rows[pl.ds(f, CHUNK), 1].reshape(n, MAIN)
        x_b = rows_b[pl.ds(f, CHUNK), 0].reshape(n, REST)
        dyp_b = rows_b[pl.ds(f, CHUNK), 1].reshape(n, REST)
        ab = dot(x, wgu[pl.ds(0, MAIN), :], ((1,), (0,))) + dot(x_b, wgu[pl.ds(MAIN, REST), :], ((1,), (0,)))
        q = dot(dyp, wdn[:, pl.ds(0, MAIN)], ((1,), (1,))) + dot(dyp_b, wdn[:, pl.ds(MAIN, REST)], ((1,), (1,)))
        a, b = ab[:, :HALF], ab[:, HALF:]
        sig = jax.nn.sigmoid(a)
        act = a * sig
        h = (act * b).astype(BF)
        part = jnp.sum(q * h.astype(F32), axis=1, keepdims=True)
        d_gate = (q * b * sig * (1.0 + a * (1.0 - sig))).astype(BF)
        d_up = (q * act).astype(BF)
        hid[pl.ds(r, n), :] = h
        dab[pl.ds(r, n), pl.ds(0, HALF)] = d_gate
        dab[pl.ds(r, n), pl.ds(HALF, HALF)] = d_up
        both = dab[pl.ds(r, n), :]
        back = dot(both, wgu[...], ((1,), (1,))).astype(BF)
        ret_out[pl.ds(f, CHUNK), :, pl.ds(0, WIDTH)] = back.reshape(CHUNK, SLOTS, WIDTH)
        high = part.astype(BF).astype(F32)
        at = lax.broadcasted_iota(jnp.int32, (n, TAIL), 1)
        tail = jnp.where(at == 0, high, jnp.where(at == 1, part - high, 0.0)).astype(BF)
        ret_out[pl.ds(f, CHUNK), :, pl.ds(WIDTH, TAIL)] = tail.reshape(CHUNK, SLOTS, TAIL)

        @pl.when(first == 0)
        def _():
            local_giveback(g).start()

        def leave(j, _):
            o = first + j

            @pl.when(o > 0)
            def _():
                giveback(g, o).start()

            return 0

        lax.fori_loop(0, CHUNK, leave, 0)
        return 0

    lax.fori_loop(0, 2 * EXPERTS // CHUNK, work, 0)

    def join(g):
        local_giveback(g).wait()

        def arrive(o, _):
            giveback(g, o).wait_recv()
            return 0

        lax.fori_loop(1, EXPERTS, arrive, 0)
        hits, _ = picks(g)
        got = ret_in.at[pl.ds(g * EXPERTS, EXPERTS)]
        mine = (hits[0] | hits[1]).astype(BF)
        dx = dot(mine, got[:, :, pl.ds(0, WIDTH)].reshape(EXPERTS * SLOTS, WIDTH), ((1,), (0,)))
        fin_out[g] = dx.astype(BF)
        final(g).start()
        tail = got[:, :, pl.ds(WIDTH, TAIL)].reshape(EXPERTS * SLOTS, TAIL)
        parts = [dot(hits[k].astype(BF), tail, ((1,), (0,))) for k in range(2)]
        return [v[:, 0:1] + v[:, 1:2] for v in parts]

    other = join(1)
    rfin_out[...] = jnp.where(lane == 0, other[0], jnp.where(lane == 1, other[1], 0.0))
    final(2).start()

    n_rows = 2 * EXPERTS * SLOTS
    tile = 256

    def grads(held, start):
        def one(t, _):
            cols = pl.ds(pl.multiple_of(t * tile, tile), tile)
            to = pl.ds(pl.multiple_of(start + t * tile, tile), tile)
            xt = held[:, 0, :, cols].reshape(n_rows, tile)
            ggu[to, :] = dot(xt, dab[...], ((0,), (0,))).astype(BF)
            dyt = held[:, 1, :, cols].reshape(n_rows, tile)
            gdn[:, to] = dot(hid[...], dyt, ((0,), (0,))).astype(BF)
            return 0

        lax.fori_loop(0, held.shape[3] // tile, one, 0)

    grads(rows, 0)
    grads(rows_b, MAIN)
    o_copies = [
        pltpu.make_async_copy(ggu.at[:, pl.ds(0, HALF)], gg_ref, o_sem.at[0]),
        pltpu.make_async_copy(ggu.at[:, pl.ds(HALF, HALF)], gu_ref, o_sem.at[1]),
        pltpu.make_async_copy(gdn, gd_ref, o_sem.at[2]),
    ]
    for c in o_copies:
        c.start()

    own = join(0)
    final(2).wait_recv()
    there = rfin_in[...]
    total = [(own[k] + there[:, k : k + 1]) / probs[k] for k in range(2)]
    lines = [jnp.sum(jnp.where(diagonal, v, 0.0), axis=0, keepdims=True) for v in total]
    which = lax.broadcasted_iota(jnp.int32, (2, TOK), 0)
    rg_ref[...] = jnp.where(which == 0, lines[0], lines[1]).astype(BF)
    final(0).wait_recv()
    final(1).wait_recv()
    summed = fin_in[0].astype(F32) + fin_in[1].astype(F32)
    up_ref[...] = jnp.where(sec == n_sec - 1, 0.0, summed).astype(BF)

    for c in z_copies:
        c.wait_send()
    for i in range(3):
        final(i).wait_send()

    def left(o, _):
        for g in range(2):
            dispatch(g, o).wait_send()
            giveback(g, o).wait_send()
        dispatch_rest(o).wait_send()
        across(o).wait_send()
        return 0

    across(0).wait_send()
    lax.fori_loop(1, EXPERTS, left, 0)
    for c in o_copies:
        c.wait()


def hand_on(*refs):
    n = len(refs) // 3
    sems = refs[-1]
    copies_in = [pltpu.make_async_copy(refs[i], refs[2 * n + i], sems.at[0, i]) for i in range(n)]
    copies_out = [pltpu.make_async_copy(refs[2 * n + i], refs[n + i], sems.at[1, i]) for i in range(n)]
    for c in copies_in:
        c.start()
    for arrived, c in zip(copies_in, copies_out):
        arrived.wait()
        c.start()
    for c in copies_out:
        c.wait()


def body(tokens, routes, probs, cotangent, w_gate, w_up, w_down):
    vmem = pl.BlockSpec(memory_space=pltpu.VMEM)
    hbm = pl.BlockSpec(memory_space=pl.ANY)
    blocks = 2 * EXPERTS
    n_rows = blocks * SLOTS
    out = pl.pallas_call(
        kernel,
        out_shape=(
            jax.ShapeDtypeStruct((TOK, WIDTH), BF),
            jax.ShapeDtypeStruct((2, TOK), BF),
            jax.ShapeDtypeStruct((WIDTH, HALF), BF),
            jax.ShapeDtypeStruct((WIDTH, HALF), BF),
            jax.ShapeDtypeStruct((HALF, WIDTH), BF),
        ),
        in_specs=[vmem, vmem, vmem, vmem, hbm, hbm, hbm],
        out_specs=(vmem, vmem, hbm, hbm, hbm),
        scratch_shapes=[
            pltpu.VMEM((WIDTH, 2 * HALF), BF),
            pltpu.VMEM((HALF, WIDTH), BF),
            pltpu.VMEM((2, TOK, MAIN), BF),
            pltpu.VMEM((2, TOK, TOK), BF),
            pltpu.VMEM((blocks, 2, SLOTS, MAIN), BF),
            pltpu.VMEM((EXPERTS, 2, SLOTS, REST), BF),
            pltpu.VMEM((blocks, 2, SLOTS, MAIN), BF),
            pltpu.VMEM((blocks, 2, SLOTS, REST), BF),
            pltpu.VMEM((n_rows, 2 * HALF), BF),
            pltpu.VMEM((n_rows, HALF), BF),
            pltpu.VMEM((blocks, SLOTS, WIDTH + TAIL), BF),
            pltpu.VMEM((blocks, SLOTS, WIDTH + TAIL), BF),
            pltpu.VMEM((WIDTH, 2 * HALF), BF),
            pltpu.VMEM((HALF, WIDTH), BF),
            pltpu.VMEM((2, TOK, WIDTH), BF),
            pltpu.VMEM((2, TOK, WIDTH), BF),
            pltpu.VMEM((TOK, TOK), F32),
            pltpu.VMEM((TOK, TOK), F32),
            pltpu.SemaphoreType.DMA((3,)),
            pltpu.SemaphoreType.DMA((3,)),
            pltpu.SemaphoreType.DMA((3,)),
            pltpu.SemaphoreType.DMA((blocks,)),
            pltpu.SemaphoreType.DMA((blocks,)),
            pltpu.SemaphoreType.DMA((EXPERTS,)),
            pltpu.SemaphoreType.DMA((EXPERTS,)),
            pltpu.SemaphoreType.DMA((EXPERTS,)),
            pltpu.SemaphoreType.DMA((EXPERTS,)),
            pltpu.SemaphoreType.DMA((blocks,)),
            pltpu.SemaphoreType.DMA((blocks,)),
            pltpu.SemaphoreType.DMA((3,)),
            pltpu.SemaphoreType.DMA((3,)),
            pltpu.SemaphoreType.DMA((2,)),
            pltpu.SemaphoreType.DMA((3,)),
        ],
        compiler_params=pltpu.CompilerParams(collective_id=0, has_side_effects=True, vmem_limit_bytes=58 << 20),
        name="expert_backward",
    )(tokens[0], routes[0].T, probs[0].T, cotangent[0], w_gate[0], w_up[0], w_down[0])
    upstream, route_grad, g_gate, g_up, g_down = pl.pallas_call(
        hand_on,
        out_shape=tuple(jax.ShapeDtypeStruct(o.shape, o.dtype) for o in out),
        in_specs=[hbm] * len(out),
        out_specs=(hbm,) * len(out),
        scratch_shapes=[pltpu.VMEM(o.shape, o.dtype) for o in out] + [pltpu.SemaphoreType.DMA((2, len(out)))],
        compiler_params=pltpu.CompilerParams(vmem_limit_bytes=58 << 20),
        name="hand_on",
    )(*out)
    return upstream[None], route_grad.T[None], g_gate[None], g_up[None], g_down[None]


def solution(mesh):
    by_token = P("section", "expert", None)
    by_column = P("section", None, "expert")
    return jax.shard_map(
        body,
        mesh=mesh,
        in_specs=(by_token, by_token, by_token, by_token, by_column, by_column, by_token),
        out_specs=(by_token, by_token, by_column, by_column, by_token),
        check_vma=False,
    )
```

```python
import jax
import jax.numpy as jnp
from jax import lax
from jax.experimental import pallas as pl
from jax.experimental.pallas import tpu as pltpu
from jax.sharding import PartitionSpec as P

BF = jnp.bfloat16
F32 = jnp.float32
SIDE = 4
EXPERTS = SIDE * SIDE
SLOTS = 32
TOK = 128
WIDTH = 2048
HALF = 384
TAIL = 128
CHUNK = 8
REST = 768
MAIN = WIDTH - REST
FAR = 1024
NEAR = WIDTH - FAR
PART = NEAR + TAIL
EARLY = 16
MESH = pl.DeviceIdType.MESH


def dot(a, b, dims):
    return lax.dot_general(a, b, (dims, ((), ())), preferred_element_type=F32)


def kernel(
    x_ref, routes_ref, probs_ref, dy_ref, wg_ref, wu_ref, wd_ref,
    up_ref, rg_ref, gg_ref, gu_ref, gd_ref,
    wgu, wdn, pair, metas, stage, stage_b, rows, rows_b, dab, hid, ret_out, ret_in, summand, ggu, gdn,
    fin_out, fin_in, rfin_out, rfin_in,
    w_sem, z_send, z_recv, d_send, d_recv, b_send, b_recv, c_send, c_recv, r_send, r_recv, f_send, f_recv, s_send, s_recv, l_sem, o_sem,
):
    sec = lax.axis_index("section")
    unit = lax.axis_index("expert")
    n_sec = lax.axis_size("section")
    zh = unit % 2
    ex = (unit // 2) % SIDE
    ey = unit // (2 * SIDE)
    mate = unit + 1 - 2 * zh
    prev = (sec + n_sec - 1) % n_sec

    def ahead(o):
        dx = o % SIDE
        dy = (o + o // SIDE) % SIDE
        return ((ey + dy) % SIDE * SIDE + (ex + dx) % SIDE) * 2 + zh

    def behind(o):
        dx = o % SIDE
        dy = (o + o // SIDE) % SIDE
        return ((ey + SIDE - dy) % SIDE * SIDE + (ex + SIDE - dx) % SIDE) * 2 + zh

    w_copies = [
        pltpu.make_async_copy(wg_ref, wgu.at[:, pl.ds(0, HALF)], w_sem.at[0]),
        pltpu.make_async_copy(wu_ref, wgu.at[:, pl.ds(HALF, HALF)], w_sem.at[1]),
        pltpu.make_async_copy(wd_ref, wdn, w_sem.at[2]),
    ]

    def to_mate(src, dst, i):
        return pltpu.make_async_remote_copy(
            src_ref=src, dst_ref=dst, send_sem=z_send.at[i], recv_sem=z_recv.at[i],
            device_id={"expert": mate}, device_id_type=MESH)

    z_copies = [
        to_mate(x_ref.at[:, pl.ds(0, MAIN)], pair.at[0], 0),
        to_mate(dy_ref.at[:, pl.ds(0, MAIN)], pair.at[1], 1),
        to_mate(metas.at[0], metas.at[1], 2),
    ]

    def dispatch(g, o):
        f = g * EXPERTS + o
        return pltpu.make_async_remote_copy(
            src_ref=stage.at[f], dst_ref=rows.at[f], send_sem=d_send.at[f], recv_sem=d_recv.at[f],
            device_id={"expert": ahead(o)}, device_id_type=MESH)

    def dispatch_rest(o):
        return pltpu.make_async_remote_copy(
            src_ref=stage_b.at[o], dst_ref=rows_b.at[o], send_sem=b_send.at[o], recv_sem=b_recv.at[o],
            device_id={"expert": ahead(o)}, device_id_type=MESH)

    def across(o):
        return pltpu.make_async_remote_copy(
            src_ref=rows_b.at[o], dst_ref=rows_b.at[EXPERTS + o], send_sem=c_send.at[o], recv_sem=c_recv.at[o],
            device_id={"expert": mate}, device_id_type=MESH)

    def giveback(g, o):
        f = g * EXPERTS + o
        return pltpu.make_async_remote_copy(
            src_ref=ret_out.at[f], dst_ref=ret_in.at[f], send_sem=r_send.at[f], recv_sem=r_recv.at[f],
            device_id={"expert": behind(o)}, device_id_type=MESH)

    def giveback_part(o):
        f = EXPERTS + o
        cols = pl.ds(0, PART)
        return pltpu.make_async_remote_copy(
            src_ref=ret_out.at[f, :, cols], dst_ref=ret_in.at[f, :, cols], send_sem=r_send.at[f],
            recv_sem=r_recv.at[f], device_id={"expert": behind(o)}, device_id_type=MESH)

    summand_copy = pltpu.make_async_remote_copy(
        src_ref=ret_out.at[pl.ds(EXPERTS + CHUNK, CHUNK), :, pl.ds(PART, FAR)], dst_ref=summand,
        send_sem=s_send, recv_sem=s_recv, device_id={"expert": mate}, device_id_type=MESH)

    def local_giveback(g):
        f = g * EXPERTS
        return pltpu.make_async_copy(ret_out.at[f], ret_in.at[f], l_sem.at[g])

    def final(i):
        src, dst = ((fin_out.at[0], fin_in.at[0]), (fin_out.at[1], fin_in.at[1]), (rfin_out, rfin_in))[i]
        to = ({"section": prev}, {"section": prev, "expert": mate}, {"expert": mate})[i]
        return pltpu.make_async_remote_copy(
            src_ref=src, dst_ref=dst, send_sem=f_send.at[i], recv_sem=f_recv.at[i],
            device_id=to, device_id_type=MESH)

    following = (sec + 1) % n_sec
    gate = pltpu.get_barrier_semaphore()
    others = [{"expert": ahead(o)} for o in range(1, EXPERTS)] + [{"expert": mate}]
    others += [{"section": s, "expert": u} for s in (prev, following) for u in (unit, mate)]
    for other in others:
        pl.semaphore_signal(gate, inc=1, device_id=other, device_id_type=MESH)
    for c in w_copies:
        c.start()

    lane = lax.broadcasted_iota(jnp.int32, (TOK, TOK), 1)
    row = lax.broadcasted_iota(jnp.int32, (TOK, TOK), 0)
    diagonal = row == lane

    def column(v):
        return jnp.sum(jnp.where(diagonal, v, 0.0), axis=1, keepdims=True)

    routes = routes_ref[...].astype(F32)
    chances = probs_ref[...].astype(F32)
    named = [column(routes[k : k + 1, :]).astype(jnp.int32) for k in range(2)]
    probs = [column(chances[k : k + 1, :]) for k in range(2)]
    member = ((named[0] == lane) | (named[1] == lane)).astype(BF)
    before = dot((lane < row).astype(BF), member, ((1,), (0,)))
    meta = jnp.zeros((TOK, TOK), F32)
    for k in range(2):
        place = jnp.sum(jnp.where(lane == named[k], before, 0.0), axis=1, keepdims=True)
        dx = (named[k] + (SIDE - ex)) % SIDE
        dy = (named[k] // SIDE + (SIDE - ey)) % SIDE
        order = dx + SIDE * ((dy + SIDE - dx) % SIDE)
        meta = jnp.where(lane == 2 * k, order.astype(F32), meta)
        meta = jnp.where(lane == 2 * k + 1, place, meta)
        meta = jnp.where(lane == 4 + k, probs[k], meta)
    metas[0] = meta.astype(BF)

    def picks(g):
        m = metas[g].astype(F32)
        slot_of = lax.broadcasted_iota(jnp.int32, (TOK, EXPERTS * SLOTS), 1)
        slots = [(m[:, 2 * k : 2 * k + 1] * SLOTS + m[:, 2 * k + 1 : 2 * k + 2]).astype(jnp.int32) for k in range(2)]
        return [slot_of == s for s in slots], [m[:, 4 + k : 5 + k] for k in range(2)]

    def masks(g):
        hits, ps = picks(g)
        ones = (hits[0] | hits[1]).astype(BF)
        scaled = (jnp.where(hits[0], ps[0], 0.0) + jnp.where(hits[1], ps[1], 0.0)).astype(BF)
        return ones, scaled

    def pack(g, half, mats, srcs, cols, out, arrived):
        take = slice(half * CHUNK * SLOTS, (half + 1) * CHUNK * SLOTS)
        base = g * EXPERTS + half * CHUNK
        for which, (mat, src) in enumerate(zip(mats, srcs)):
            got = dot(mat[:, take], src[:, cols], ((0,), (0,))).astype(BF)
            got = got.reshape(CHUNK, SLOTS, got.shape[1])
            out[pl.ds(base, CHUNK), which] = got
            if half == 0:
                arrived[base, which] = got[0]

    def send(g, lo, hi):
        for o in range(max(lo, 1), hi):
            dispatch(g, o).start()

    own_masks = masks(0)
    for half in range(EXPERTS // CHUNK):
        pack(0, half, own_masks, (x_ref, dy_ref), pl.ds(MAIN, REST), stage_b, rows_b)
    pack(0, 0, own_masks, (x_ref, dy_ref), pl.ds(0, MAIN), stage, rows)

    pl.semaphore_wait(gate, len(others))
    for c in z_copies:
        c.start()
    across(0).start()
    for o in range(1, EXPERTS):
        dispatch_rest(o).start()
    send(0, 0, CHUNK)
    pack(0, 1, own_masks, (x_ref, dy_ref), pl.ds(0, MAIN), stage, rows)
    send(0, CHUNK, EARLY)

    def pass_on(o, _):
        dispatch_rest(o).wait_recv()
        across(o).start()
        return 0

    lax.fori_loop(1, EXPERTS, pass_on, 0)
    for c in z_copies:
        c.wait_recv()
    mate_masks = masks(1)
    for half in range(EXPERTS // CHUNK):
        pack(1, half, mate_masks, (pair.at[0], pair.at[1]), pl.ds(0, MAIN), stage, rows)
        send(1, half * CHUNK, (half + 1) * CHUNK)
    send(0, EARLY, EXPERTS)
    for c in w_copies:
        c.wait()

    def work(i, _):
        g = (i + 1) // 2 % 2
        first = i // 2 * CHUNK

        def arrive(j, _):
            o = first + j

            @pl.when(o > 0)
            def _():
                dispatch(g, o).wait_recv()

            @pl.when(g == 1)
            def _():
                across(o).wait_recv()

            return 0

        lax.fori_loop(0, CHUNK, arrive, 0)
        f = pl.multiple_of(g * EXPERTS + first, CHUNK)
        r = pl.multiple_of(f * SLOTS, CHUNK * SLOTS)
        n = CHUNK * SLOTS
        x = rows[pl.ds(f, CHUNK), 0].reshape(n, MAIN)
        dyp = rows[pl.ds(f, CHUNK), 1].reshape(n, MAIN)
        x_b = rows_b[pl.ds(f, CHUNK), 0].reshape(n, REST)
        dyp_b = rows_b[pl.ds(f, CHUNK), 1].reshape(n, REST)
        ab = dot(x, wgu[pl.ds(0, MAIN), :], ((1,), (0,))) + dot(x_b, wgu[pl.ds(MAIN, REST), :], ((1,), (0,)))
        q = dot(dyp, wdn[:, pl.ds(0, MAIN)], ((1,), (1,))) + dot(dyp_b, wdn[:, pl.ds(MAIN, REST)], ((1,), (1,)))
        a, b = ab[:, :HALF], ab[:, HALF:]
        sig = jax.nn.sigmoid(a)
        act = a * sig
        h = (act * b).astype(BF)
        part = jnp.sum(q * h.astype(F32), axis=1, keepdims=True)
        d_gate = (q * b * sig * (1.0 + a * (1.0 - sig))).astype(BF)
        d_up = (q * act).astype(BF)
        hid[pl.ds(r, n), :] = h
        dab[pl.ds(r, n), pl.ds(0, HALF)] = d_gate
        dab[pl.ds(r, n), pl.ds(HALF, HALF)] = d_up
        both = dab[pl.ds(r, n), :]
        back = dot(both, wgu[...], ((1,), (1,)))
        ret_out[pl.ds(f, CHUNK), :, pl.ds(0, NEAR)] = back[:, :NEAR].astype(BF).reshape(CHUNK, SLOTS, NEAR)
        far = back[:, NEAR:]

        @pl.when(i < 3)
        def _():
            ret_out[pl.ds(f, CHUNK), :, pl.ds(PART, FAR)] = far.astype(BF).reshape(CHUNK, SLOTS, FAR)

        @pl.when(i == 2)
        def _():
            summand_copy.start()

        @pl.when(i == 3)
        def _():
            summand_copy.wait_recv()
            both_halves = far + summand[...].reshape(n, FAR).astype(F32)
            ret_out[pl.ds(f, CHUNK), :, pl.ds(PART, FAR)] = both_halves.astype(BF).reshape(CHUNK, SLOTS, FAR)

        high = part.astype(BF).astype(F32)
        at = lax.broadcasted_iota(jnp.int32, (n, TAIL), 1)
        tail = jnp.where(at == 0, high, jnp.where(at == 1, part - high, 0.0)).astype(BF)
        ret_out[pl.ds(f, CHUNK), :, pl.ds(NEAR, TAIL)] = tail.reshape(CHUNK, SLOTS, TAIL)

        @pl.when(first == 0)
        def _():
            local_giveback(g).start()

        def leave(j, _):
            o = first + j

            @pl.when((o > 0) & (i != 2))
            def _():
                giveback(g, o).start()

            @pl.when(i == 2)
            def _():
                giveback_part(o).start()

            return 0

        lax.fori_loop(0, CHUNK, leave, 0)
        return 0

    lax.fori_loop(0, 2 * EXPERTS // CHUNK, work, 0)

    def join(g):
        local_giveback(g).wait()

        whole = EXPERTS if g == 0 else CHUNK

        def arrive(o, _):
            giveback(g, o).wait_recv()
            return 0

        def arrive_part(o, _):
            giveback_part(o).wait_recv()
            return 0

        lax.fori_loop(1, whole, arrive, 0)
        lax.fori_loop(whole, EXPERTS, arrive_part, 0)
        hits, _ = picks(g)
        got = ret_in.at[pl.ds(g * EXPERTS, EXPERTS)]
        mine = (hits[0] | hits[1]).astype(BF)
        near = got[:, :, pl.ds(0, NEAR)].reshape(EXPERTS * SLOTS, NEAR)
        fin_out[g, :, pl.ds(0, NEAR)] = dot(mine, near, ((1,), (0,))).astype(BF)
        far = got[pl.ds(0, whole), :, pl.ds(PART, FAR)].reshape(whole * SLOTS, FAR)
        fin_out[g, :, pl.ds(NEAR, FAR)] = dot(mine[:, : whole * SLOTS], far, ((1,), (0,))).astype(BF)
        final(g).start()
        tail = got[:, :, pl.ds(NEAR, TAIL)].reshape(EXPERTS * SLOTS, TAIL)
        parts = [dot(hits[k].astype(BF), tail, ((1,), (0,))) for k in range(2)]
        return [v[:, 0:1] + v[:, 1:2] for v in parts]

    other = join(1)
    rfin_out[...] = jnp.where(lane == 0, other[0], jnp.where(lane == 1, other[1], 0.0))
    final(2).start()

    n_rows = 2 * EXPERTS * SLOTS
    tile = 256

    def grads(held, start):
        def one(t, _):
            cols = pl.ds(pl.multiple_of(t * tile, tile), tile)
            to = pl.ds(pl.multiple_of(start + t * tile, tile), tile)
            xt = held[:, 0, :, cols].reshape(n_rows, tile)
            ggu[to, :] = dot(xt, dab[...], ((0,), (0,))).astype(BF)
            dyt = held[:, 1, :, cols].reshape(n_rows, tile)
            gdn[:, to] = dot(hid[...], dyt, ((0,), (0,))).astype(BF)
            return 0

        lax.fori_loop(0, held.shape[3] // tile, one, 0)

    grads(rows, 0)
    grads(rows_b, MAIN)
    o_copies = [
        pltpu.make_async_copy(ggu.at[:, pl.ds(0, HALF)], gg_ref, o_sem.at[0]),
        pltpu.make_async_copy(ggu.at[:, pl.ds(HALF, HALF)], gu_ref, o_sem.at[1]),
        pltpu.make_async_copy(gdn, gd_ref, o_sem.at[2]),
    ]
    for c in o_copies:
        c.start()

    own = join(0)
    final(2).wait_recv()
    there = rfin_in[...]
    total = [(own[k] + there[:, k : k + 1]) / probs[k] for k in range(2)]
    lines = [jnp.sum(jnp.where(diagonal, v, 0.0), axis=0, keepdims=True) for v in total]
    which = lax.broadcasted_iota(jnp.int32, (2, TOK), 0)
    rg_ref[...] = jnp.where(which == 0, lines[0], lines[1]).astype(BF)
    final(0).wait_recv()
    final(1).wait_recv()
    summed = fin_in[0].astype(F32) + fin_in[1].astype(F32)
    up_ref[...] = jnp.where(sec == n_sec - 1, 0.0, summed).astype(BF)

    for c in z_copies:
        c.wait_send()
    for i in range(3):
        final(i).wait_send()

    summand_copy.wait_send()
    across(0).wait_send()

    def left(o, _):
        for g in range(2):
            dispatch(g, o).wait_send()
        dispatch_rest(o).wait_send()
        across(o).wait_send()
        giveback(0, o).wait_send()

        @pl.when(o < CHUNK)
        def _():
            giveback(1, o).wait_send()

        @pl.when(o >= CHUNK)
        def _():
            giveback_part(o).wait_send()

        return 0

    lax.fori_loop(1, EXPERTS, left, 0)
    for c in o_copies:
        c.wait()


def hand_on(*refs):
    n = len(refs) // 3
    sems = refs[-1]
    copies_in = [pltpu.make_async_copy(refs[i], refs[2 * n + i], sems.at[0, i]) for i in range(n)]
    copies_out = [pltpu.make_async_copy(refs[2 * n + i], refs[n + i], sems.at[1, i]) for i in range(n)]
    for c in copies_in:
        c.start()
    for arrived, c in zip(copies_in, copies_out):
        arrived.wait()
        c.start()
    for c in copies_out:
        c.wait()


def body(tokens, routes, probs, cotangent, w_gate, w_up, w_down):
    vmem = pl.BlockSpec(memory_space=pltpu.VMEM)
    hbm = pl.BlockSpec(memory_space=pl.ANY)
    blocks = 2 * EXPERTS
    n_rows = blocks * SLOTS
    out = pl.pallas_call(
        kernel,
        out_shape=(
            jax.ShapeDtypeStruct((TOK, WIDTH), BF),
            jax.ShapeDtypeStruct((2, TOK), BF),
            jax.ShapeDtypeStruct((WIDTH, HALF), BF),
            jax.ShapeDtypeStruct((WIDTH, HALF), BF),
            jax.ShapeDtypeStruct((HALF, WIDTH), BF),
        ),
        in_specs=[vmem, vmem, vmem, vmem, hbm, hbm, hbm],
        out_specs=(vmem, vmem, hbm, hbm, hbm),
        scratch_shapes=[
            pltpu.VMEM((WIDTH, 2 * HALF), BF),
            pltpu.VMEM((HALF, WIDTH), BF),
            pltpu.VMEM((2, TOK, MAIN), BF),
            pltpu.VMEM((2, TOK, TOK), BF),
            pltpu.VMEM((blocks, 2, SLOTS, MAIN), BF),
            pltpu.VMEM((EXPERTS, 2, SLOTS, REST), BF),
            pltpu.VMEM((blocks, 2, SLOTS, MAIN), BF),
            pltpu.VMEM((blocks, 2, SLOTS, REST), BF),
            pltpu.VMEM((n_rows, 2 * HALF), BF),
            pltpu.VMEM((n_rows, HALF), BF),
            pltpu.VMEM((blocks, SLOTS, WIDTH + TAIL), BF),
            pltpu.VMEM((blocks, SLOTS, WIDTH + TAIL), BF),
            pltpu.VMEM((CHUNK, SLOTS, FAR), BF),
            pltpu.VMEM((WIDTH, 2 * HALF), BF),
            pltpu.VMEM((HALF, WIDTH), BF),
            pltpu.VMEM((2, TOK, WIDTH), BF),
            pltpu.VMEM((2, TOK, WIDTH), BF),
            pltpu.VMEM((TOK, TOK), F32),
            pltpu.VMEM((TOK, TOK), F32),
            pltpu.SemaphoreType.DMA((3,)),
            pltpu.SemaphoreType.DMA((3,)),
            pltpu.SemaphoreType.DMA((3,)),
            pltpu.SemaphoreType.DMA((blocks,)),
            pltpu.SemaphoreType.DMA((blocks,)),
            pltpu.SemaphoreType.DMA((EXPERTS,)),
            pltpu.SemaphoreType.DMA((EXPERTS,)),
            pltpu.SemaphoreType.DMA((EXPERTS,)),
            pltpu.SemaphoreType.DMA((EXPERTS,)),
            pltpu.SemaphoreType.DMA((blocks,)),
            pltpu.SemaphoreType.DMA((blocks,)),
            pltpu.SemaphoreType.DMA((3,)),
            pltpu.SemaphoreType.DMA((3,)),
            pltpu.SemaphoreType.DMA,
            pltpu.SemaphoreType.DMA,
            pltpu.SemaphoreType.DMA((2,)),
            pltpu.SemaphoreType.DMA((3,)),
        ],
        compiler_params=pltpu.CompilerParams(collective_id=0, has_side_effects=True, vmem_limit_bytes=58 << 20),
        name="expert_backward",
    )(tokens[0], routes[0].T, probs[0].T, cotangent[0], w_gate[0], w_up[0], w_down[0])
    upstream, route_grad, g_gate, g_up, g_down = pl.pallas_call(
        hand_on,
        out_shape=tuple(jax.ShapeDtypeStruct(o.shape, o.dtype) for o in out),
        in_specs=[hbm] * len(out),
        out_specs=(hbm,) * len(out),
        scratch_shapes=[pltpu.VMEM(o.shape, o.dtype) for o in out] + [pltpu.SemaphoreType.DMA((2, len(out)))],
        compiler_params=pltpu.CompilerParams(vmem_limit_bytes=58 << 20),
        name="hand_on",
    )(*out)
    return upstream[None], route_grad.T[None], g_gate[None], g_up[None], g_down[None]


def solution(mesh):
    by_token = P("section", "expert", None)
    by_column = P("section", None, "expert")
    return jax.shard_map(
        body,
        mesh=mesh,
        in_specs=(by_token, by_token, by_token, by_token, by_column, by_column, by_token),
        out_specs=(by_token, by_token, by_column, by_column, by_token),
        check_vma=False,
    )
```

```python
import jax
import jax.numpy as jnp
from jax import lax
from jax.experimental import pallas as pl
from jax.experimental.pallas import tpu as pltpu
from jax.sharding import PartitionSpec as P

BF = jnp.bfloat16
F32 = jnp.float32
SIDE = 4
EXPERTS = SIDE * SIDE
SLOTS = 32
TOK = 128
WIDTH = 2048
HALF = 384
TAIL = 128
CHUNK = 8
REST = 768
MAIN = WIDTH - REST
FAR = 640
NEAR = WIDTH - FAR
PART = NEAR + TAIL
EARLY = 16
MESH = pl.DeviceIdType.MESH


def dot(a, b, dims):
    return lax.dot_general(a, b, (dims, ((), ())), preferred_element_type=F32)


def kernel(
    x_ref, routes_ref, probs_ref, dy_ref, wg_ref, wu_ref, wd_ref,
    up_ref, rg_ref, gg_ref, gu_ref, gd_ref,
    wgu, wdn, pair, metas, stage, stage_b, rows, rows_b, dab, hid, ret_out, ret_in, summand, ggu, gdn,
    fin_out, fin_in, rfin_out, rfin_in,
    w_sem, z_send, z_recv, d_send, d_recv, b_send, b_recv, c_send, c_recv, r_send, r_recv, f_send, f_recv, s_send, s_recv, l_sem, o_sem,
):
    sec = lax.axis_index("section")
    unit = lax.axis_index("expert")
    n_sec = lax.axis_size("section")
    zh = unit % 2
    ex = (unit // 2) % SIDE
    ey = unit // (2 * SIDE)
    mate = unit + 1 - 2 * zh
    prev = (sec + n_sec - 1) % n_sec

    def ahead(o):
        dx = o % SIDE
        dy = (o + o // SIDE) % SIDE
        return ((ey + dy) % SIDE * SIDE + (ex + dx) % SIDE) * 2 + zh

    def behind(o):
        dx = o % SIDE
        dy = (o + o // SIDE) % SIDE
        return ((ey + SIDE - dy) % SIDE * SIDE + (ex + SIDE - dx) % SIDE) * 2 + zh

    w_copies = [
        pltpu.make_async_copy(wg_ref, wgu.at[:, pl.ds(0, HALF)], w_sem.at[0]),
        pltpu.make_async_copy(wu_ref, wgu.at[:, pl.ds(HALF, HALF)], w_sem.at[1]),
        pltpu.make_async_copy(wd_ref, wdn, w_sem.at[2]),
    ]

    def to_mate(src, dst, i):
        return pltpu.make_async_remote_copy(
            src_ref=src, dst_ref=dst, send_sem=z_send.at[i], recv_sem=z_recv.at[i],
            device_id={"expert": mate}, device_id_type=MESH)

    z_copies = [
        to_mate(x_ref.at[:, pl.ds(0, MAIN)], pair.at[0], 0),
        to_mate(dy_ref.at[:, pl.ds(0, MAIN)], pair.at[1], 1),
        to_mate(metas.at[0], metas.at[1], 2),
    ]

    def dispatch(g, o):
        f = g * EXPERTS + o
        return pltpu.make_async_remote_copy(
            src_ref=stage.at[f], dst_ref=rows.at[f], send_sem=d_send.at[f], recv_sem=d_recv.at[f],
            device_id={"expert": ahead(o)}, device_id_type=MESH)

    def dispatch_rest(o):
        return pltpu.make_async_remote_copy(
            src_ref=stage_b.at[o], dst_ref=rows_b.at[o], send_sem=b_send.at[o], recv_sem=b_recv.at[o],
            device_id={"expert": ahead(o)}, device_id_type=MESH)

    def across(o):
        return pltpu.make_async_remote_copy(
            src_ref=rows_b.at[o], dst_ref=rows_b.at[EXPERTS + o], send_sem=c_send.at[o], recv_sem=c_recv.at[o],
            device_id={"expert": mate}, device_id_type=MESH)

    def giveback(g, o):
        f = g * EXPERTS + o
        return pltpu.make_async_remote_copy(
            src_ref=ret_out.at[f], dst_ref=ret_in.at[f], send_sem=r_send.at[f], recv_sem=r_recv.at[f],
            device_id={"expert": behind(o)}, device_id_type=MESH)

    def giveback_part(o):
        f = EXPERTS + o
        cols = pl.ds(0, PART)
        return pltpu.make_async_remote_copy(
            src_ref=ret_out.at[f, :, cols], dst_ref=ret_in.at[f, :, cols], send_sem=r_send.at[f],
            recv_sem=r_recv.at[f], device_id={"expert": behind(o)}, device_id_type=MESH)

    summand_copy = pltpu.make_async_remote_copy(
        src_ref=ret_out.at[pl.ds(EXPERTS + CHUNK, CHUNK), :, pl.ds(PART, FAR)], dst_ref=summand,
        send_sem=s_send, recv_sem=s_recv, device_id={"expert": mate}, device_id_type=MESH)

    def local_giveback(g):
        f = g * EXPERTS
        return pltpu.make_async_copy(ret_out.at[f], ret_in.at[f], l_sem.at[g])

    def final(i):
        src, dst = ((fin_out.at[0], fin_in.at[0]), (fin_out.at[1], fin_in.at[1]), (rfin_out, rfin_in))[i]
        to = ({"section": prev}, {"section": prev, "expert": mate}, {"expert": mate})[i]
        return pltpu.make_async_remote_copy(
            src_ref=src, dst_ref=dst, send_sem=f_send.at[i], recv_sem=f_recv.at[i],
            device_id=to, device_id_type=MESH)

    following = (sec + 1) % n_sec
    gate = pltpu.get_barrier_semaphore()
    others = [{"expert": ahead(o)} for o in range(1, EXPERTS)] + [{"expert": mate}]
    others += [{"section": s, "expert": u} for s in (prev, following) for u in (unit, mate)]
    for other in others:
        pl.semaphore_signal(gate, inc=1, device_id=other, device_id_type=MESH)
    for c in w_copies:
        c.start()

    lane = lax.broadcasted_iota(jnp.int32, (TOK, TOK), 1)
    row = lax.broadcasted_iota(jnp.int32, (TOK, TOK), 0)
    diagonal = row == lane

    def column(v):
        return jnp.sum(jnp.where(diagonal, v, 0.0), axis=1, keepdims=True)

    routes = routes_ref[...].astype(F32)
    chances = probs_ref[...].astype(F32)
    named = [column(routes[k : k + 1, :]).astype(jnp.int32) for k in range(2)]
    probs = [column(chances[k : k + 1, :]) for k in range(2)]
    member = ((named[0] == lane) | (named[1] == lane)).astype(BF)
    before = dot((lane < row).astype(BF), member, ((1,), (0,)))
    meta = jnp.zeros((TOK, TOK), F32)
    for k in range(2):
        place = jnp.sum(jnp.where(lane == named[k], before, 0.0), axis=1, keepdims=True)
        dx = (named[k] + (SIDE - ex)) % SIDE
        dy = (named[k] // SIDE + (SIDE - ey)) % SIDE
        order = dx + SIDE * ((dy + SIDE - dx) % SIDE)
        meta = jnp.where(lane == 2 * k, order.astype(F32), meta)
        meta = jnp.where(lane == 2 * k + 1, place, meta)
        meta = jnp.where(lane == 4 + k, probs[k], meta)
    metas[0] = meta.astype(BF)

    def picks(g):
        m = metas[g].astype(F32)
        slot_of = lax.broadcasted_iota(jnp.int32, (TOK, EXPERTS * SLOTS), 1)
        slots = [(m[:, 2 * k : 2 * k + 1] * SLOTS + m[:, 2 * k + 1 : 2 * k + 2]).astype(jnp.int32) for k in range(2)]
        return [slot_of == s for s in slots], [m[:, 4 + k : 5 + k] for k in range(2)]

    def masks(g):
        hits, ps = picks(g)
        ones = (hits[0] | hits[1]).astype(BF)
        scaled = (jnp.where(hits[0], ps[0], 0.0) + jnp.where(hits[1], ps[1], 0.0)).astype(BF)
        return ones, scaled

    def pack(g, half, mats, srcs, cols, out, arrived):
        take = slice(half * CHUNK * SLOTS, (half + 1) * CHUNK * SLOTS)
        base = g * EXPERTS + half * CHUNK
        for which, (mat, src) in enumerate(zip(mats, srcs)):
            got = dot(mat[:, take], src[:, cols], ((0,), (0,))).astype(BF)
            got = got.reshape(CHUNK, SLOTS, got.shape[1])
            out[pl.ds(base, CHUNK), which] = got
            if half == 0:
                arrived[base, which] = got[0]

    def send(g, lo, hi):
        for o in range(max(lo, 1), hi):
            dispatch(g, o).start()

    own_masks = masks(0)
    for half in range(EXPERTS // CHUNK):
        pack(0, half, own_masks, (x_ref, dy_ref), pl.ds(MAIN, REST), stage_b, rows_b)
    pack(0, 0, own_masks, (x_ref, dy_ref), pl.ds(0, MAIN), stage, rows)

    pl.semaphore_wait(gate, len(others))
    for c in z_copies:
        c.start()
    across(0).start()
    for o in range(1, EXPERTS):
        dispatch_rest(o).start()
    send(0, 0, CHUNK)
    pack(0, 1, own_masks, (x_ref, dy_ref), pl.ds(0, MAIN), stage, rows)
    send(0, CHUNK, EARLY)

    def pass_on(o, _):
        dispatch_rest(o).wait_recv()
        across(o).start()
        return 0

    lax.fori_loop(1, EXPERTS, pass_on, 0)
    for c in z_copies:
        c.wait_recv()
    mate_masks = masks(1)
    for half in range(EXPERTS // CHUNK):
        pack(1, half, mate_masks, (pair.at[0], pair.at[1]), pl.ds(0, MAIN), stage, rows)
        send(1, half * CHUNK, (half + 1) * CHUNK)
    send(0, EARLY, EXPERTS)
    for c in w_copies:
        c.wait()

    def work(i, _):
        g = (i + 1) // 2 % 2
        first = i // 2 * CHUNK

        def arrive(j, _):
            o = first + j

            @pl.when(o > 0)
            def _():
                dispatch(g, o).wait_recv()

            @pl.when(g == 1)
            def _():
                across(o).wait_recv()

            return 0

        lax.fori_loop(0, CHUNK, arrive, 0)
        f = pl.multiple_of(g * EXPERTS + first, CHUNK)
        r = pl.multiple_of(f * SLOTS, CHUNK * SLOTS)
        n = CHUNK * SLOTS
        x = rows[pl.ds(f, CHUNK), 0].reshape(n, MAIN)
        dyp = rows[pl.ds(f, CHUNK), 1].reshape(n, MAIN)
        x_b = rows_b[pl.ds(f, CHUNK), 0].reshape(n, REST)
        dyp_b = rows_b[pl.ds(f, CHUNK), 1].reshape(n, REST)
        ab = dot(x, wgu[pl.ds(0, MAIN), :], ((1,), (0,))) + dot(x_b, wgu[pl.ds(MAIN, REST), :], ((1,), (0,)))
        q = dot(dyp, wdn[:, pl.ds(0, MAIN)], ((1,), (1,))) + dot(dyp_b, wdn[:, pl.ds(MAIN, REST)], ((1,), (1,)))
        a, b = ab[:, :HALF], ab[:, HALF:]
        sig = jax.nn.sigmoid(a)
        act = a * sig
        h = (act * b).astype(BF)
        part = jnp.sum(q * h.astype(F32), axis=1, keepdims=True)
        d_gate = (q * b * sig * (1.0 + a * (1.0 - sig))).astype(BF)
        d_up = (q * act).astype(BF)
        hid[pl.ds(r, n), :] = h
        dab[pl.ds(r, n), pl.ds(0, HALF)] = d_gate
        dab[pl.ds(r, n), pl.ds(HALF, HALF)] = d_up
        both = dab[pl.ds(r, n), :]
        back = dot(both, wgu[...], ((1,), (1,)))
        ret_out[pl.ds(f, CHUNK), :, pl.ds(0, NEAR)] = back[:, :NEAR].astype(BF).reshape(CHUNK, SLOTS, NEAR)
        far = back[:, NEAR:]

        @pl.when(i < 3)
        def _():
            ret_out[pl.ds(f, CHUNK), :, pl.ds(PART, FAR)] = far.astype(BF).reshape(CHUNK, SLOTS, FAR)

        @pl.when(i == 2)
        def _():
            summand_copy.start()

        @pl.when(i == 3)
        def _():
            summand_copy.wait_recv()
            both_halves = far + summand[...].reshape(n, FAR).astype(F32)
            ret_out[pl.ds(f, CHUNK), :, pl.ds(PART, FAR)] = both_halves.astype(BF).reshape(CHUNK, SLOTS, FAR)

        high = part.astype(BF).astype(F32)
        at = lax.broadcasted_iota(jnp.int32, (n, TAIL), 1)
        tail = jnp.where(at == 0, high, jnp.where(at == 1, part - high, 0.0)).astype(BF)
        ret_out[pl.ds(f, CHUNK), :, pl.ds(NEAR, TAIL)] = tail.reshape(CHUNK, SLOTS, TAIL)

        @pl.when(first == 0)
        def _():
            local_giveback(g).start()

        def leave(j, _):
            o = first + j

            @pl.when((o > 0) & (i != 2))
            def _():
                giveback(g, o).start()

            @pl.when(i == 2)
            def _():
                giveback_part(o).start()

            return 0

        lax.fori_loop(0, CHUNK, leave, 0)
        return 0

    lax.fori_loop(0, 2 * EXPERTS // CHUNK, work, 0)

    def join(g):
        local_giveback(g).wait()

        whole = EXPERTS if g == 0 else CHUNK

        def arrive(o, _):
            giveback(g, o).wait_recv()
            return 0

        def arrive_part(o, _):
            giveback_part(o).wait_recv()
            return 0

        lax.fori_loop(1, whole, arrive, 0)
        lax.fori_loop(whole, EXPERTS, arrive_part, 0)
        hits, _ = picks(g)
        got = ret_in.at[pl.ds(g * EXPERTS, EXPERTS)]
        mine = (hits[0] | hits[1]).astype(BF)
        near = got[:, :, pl.ds(0, NEAR)].reshape(EXPERTS * SLOTS, NEAR)
        fin_out[g, :, pl.ds(0, NEAR)] = dot(mine, near, ((1,), (0,))).astype(BF)
        far = got[pl.ds(0, whole), :, pl.ds(PART, FAR)].reshape(whole * SLOTS, FAR)
        fin_out[g, :, pl.ds(NEAR, FAR)] = dot(mine[:, : whole * SLOTS], far, ((1,), (0,))).astype(BF)
        final(g).start()
        tail = got[:, :, pl.ds(NEAR, TAIL)].reshape(EXPERTS * SLOTS, TAIL)
        parts = [dot(hits[k].astype(BF), tail, ((1,), (0,))) for k in range(2)]
        return [v[:, 0:1] + v[:, 1:2] for v in parts]

    other = join(1)
    rfin_out[...] = jnp.where(lane == 0, other[0], jnp.where(lane == 1, other[1], 0.0))
    final(2).start()

    n_rows = 2 * EXPERTS * SLOTS
    tile = 256

    def grads(held, start):
        def one(t, _):
            cols = pl.ds(pl.multiple_of(t * tile, tile), tile)
            to = pl.ds(pl.multiple_of(start + t * tile, tile), tile)
            xt = held[:, 0, :, cols].reshape(n_rows, tile)
            ggu[to, :] = dot(xt, dab[...], ((0,), (0,))).astype(BF)
            dyt = held[:, 1, :, cols].reshape(n_rows, tile)
            gdn[:, to] = dot(hid[...], dyt, ((0,), (0,))).astype(BF)
            return 0

        lax.fori_loop(0, held.shape[3] // tile, one, 0)

    grads(rows, 0)
    grads(rows_b, MAIN)
    o_copies = [
        pltpu.make_async_copy(ggu.at[:, pl.ds(0, HALF)], gg_ref, o_sem.at[0]),
        pltpu.make_async_copy(ggu.at[:, pl.ds(HALF, HALF)], gu_ref, o_sem.at[1]),
        pltpu.make_async_copy(gdn, gd_ref, o_sem.at[2]),
    ]
    for c in o_copies:
        c.start()

    own = join(0)
    final(2).wait_recv()
    there = rfin_in[...]
    total = [(own[k] + there[:, k : k + 1]) / probs[k] for k in range(2)]
    lines = [jnp.sum(jnp.where(diagonal, v, 0.0), axis=0, keepdims=True) for v in total]
    which = lax.broadcasted_iota(jnp.int32, (2, TOK), 0)
    rg_ref[...] = jnp.where(which == 0, lines[0], lines[1]).astype(BF)
    final(0).wait_recv()
    final(1).wait_recv()
    summed = fin_in[0].astype(F32) + fin_in[1].astype(F32)
    up_ref[...] = jnp.where(sec == n_sec - 1, 0.0, summed).astype(BF)

    for c in z_copies:
        c.wait_send()
    for i in range(3):
        final(i).wait_send()

    summand_copy.wait_send()
    across(0).wait_send()

    def left(o, _):
        for g in range(2):
            dispatch(g, o).wait_send()
        dispatch_rest(o).wait_send()
        across(o).wait_send()
        giveback(0, o).wait_send()

        @pl.when(o < CHUNK)
        def _():
            giveback(1, o).wait_send()

        @pl.when(o >= CHUNK)
        def _():
            giveback_part(o).wait_send()

        return 0

    lax.fori_loop(1, EXPERTS, left, 0)
    for c in o_copies:
        c.wait()


def hand_on(*refs):
    n = len(refs) // 3
    sems = refs[-1]
    copies_in = [pltpu.make_async_copy(refs[i], refs[2 * n + i], sems.at[0, i]) for i in range(n)]
    copies_out = [pltpu.make_async_copy(refs[2 * n + i], refs[n + i], sems.at[1, i]) for i in range(n)]
    for c in copies_in:
        c.start()
    for arrived, c in zip(copies_in, copies_out):
        arrived.wait()
        c.start()
    for c in copies_out:
        c.wait()


def body(tokens, routes, probs, cotangent, w_gate, w_up, w_down):
    vmem = pl.BlockSpec(memory_space=pltpu.VMEM)
    hbm = pl.BlockSpec(memory_space=pl.ANY)
    blocks = 2 * EXPERTS
    n_rows = blocks * SLOTS
    out = pl.pallas_call(
        kernel,
        out_shape=(
            jax.ShapeDtypeStruct((TOK, WIDTH), BF),
            jax.ShapeDtypeStruct((2, TOK), BF),
            jax.ShapeDtypeStruct((WIDTH, HALF), BF),
            jax.ShapeDtypeStruct((WIDTH, HALF), BF),
            jax.ShapeDtypeStruct((HALF, WIDTH), BF),
        ),
        in_specs=[vmem, vmem, vmem, vmem, hbm, hbm, hbm],
        out_specs=(vmem, vmem, hbm, hbm, hbm),
        scratch_shapes=[
            pltpu.VMEM((WIDTH, 2 * HALF), BF),
            pltpu.VMEM((HALF, WIDTH), BF),
            pltpu.VMEM((2, TOK, MAIN), BF),
            pltpu.VMEM((2, TOK, TOK), BF),
            pltpu.VMEM((blocks, 2, SLOTS, MAIN), BF),
            pltpu.VMEM((EXPERTS, 2, SLOTS, REST), BF),
            pltpu.VMEM((blocks, 2, SLOTS, MAIN), BF),
            pltpu.VMEM((blocks, 2, SLOTS, REST), BF),
            pltpu.VMEM((n_rows, 2 * HALF), BF),
            pltpu.VMEM((n_rows, HALF), BF),
            pltpu.VMEM((blocks, SLOTS, WIDTH + TAIL), BF),
            pltpu.VMEM((blocks, SLOTS, WIDTH + TAIL), BF),
            pltpu.VMEM((CHUNK, SLOTS, FAR), BF),
            pltpu.VMEM((WIDTH, 2 * HALF), BF),
            pltpu.VMEM((HALF, WIDTH), BF),
            pltpu.VMEM((2, TOK, WIDTH), BF),
            pltpu.VMEM((2, TOK, WIDTH), BF),
            pltpu.VMEM((TOK, TOK), F32),
            pltpu.VMEM((TOK, TOK), F32),
            pltpu.SemaphoreType.DMA((3,)),
            pltpu.SemaphoreType.DMA((3,)),
            pltpu.SemaphoreType.DMA((3,)),
            pltpu.SemaphoreType.DMA((blocks,)),
            pltpu.SemaphoreType.DMA((blocks,)),
            pltpu.SemaphoreType.DMA((EXPERTS,)),
            pltpu.SemaphoreType.DMA((EXPERTS,)),
            pltpu.SemaphoreType.DMA((EXPERTS,)),
            pltpu.SemaphoreType.DMA((EXPERTS,)),
            pltpu.SemaphoreType.DMA((blocks,)),
            pltpu.SemaphoreType.DMA((blocks,)),
            pltpu.SemaphoreType.DMA((3,)),
            pltpu.SemaphoreType.DMA((3,)),
            pltpu.SemaphoreType.DMA,
            pltpu.SemaphoreType.DMA,
            pltpu.SemaphoreType.DMA((2,)),
            pltpu.SemaphoreType.DMA((3,)),
        ],
        compiler_params=pltpu.CompilerParams(collective_id=0, has_side_effects=True, vmem_limit_bytes=58 << 20),
        name="expert_backward",
    )(tokens[0], routes[0].T, probs[0].T, cotangent[0], w_gate[0], w_up[0], w_down[0])
    upstream, route_grad, g_gate, g_up, g_down = pl.pallas_call(
        hand_on,
        out_shape=tuple(jax.ShapeDtypeStruct(o.shape, o.dtype) for o in out),
        in_specs=[hbm] * len(out),
        out_specs=(hbm,) * len(out),
        scratch_shapes=[pltpu.VMEM(o.shape, o.dtype) for o in out] + [pltpu.SemaphoreType.DMA((2, len(out)))],
        compiler_params=pltpu.CompilerParams(vmem_limit_bytes=58 << 20),
        name="hand_on",
    )(*out)
    return upstream[None], route_grad.T[None], g_gate[None], g_up[None], g_down[None]


def solution(mesh):
    by_token = P("section", "expert", None)
    by_column = P("section", None, "expert")
    return jax.shard_map(
        body,
        mesh=mesh,
        in_specs=(by_token, by_token, by_token, by_token, by_column, by_column, by_token),
        out_specs=(by_token, by_token, by_column, by_column, by_token),
        check_vma=False,
    )
```
